32 devices in a mesh: gx: 8 (over z, core), gy: 4 (over y, x).
Axes of the slice: x: 2, y: 2, z: 4, core: 2. Of those that a mesh axis runs over, the one named last changes fastest.
Arguments:
- velocity: float32 [2, 512, 1024], P(None, 'gy', 'gx'), may hold values from -6 to 6
- wind_stress: float32 [2, 512, 1024], P(None, 'gy', 'gx'), may hold values from -6 to 6
- thickness: float32 [512, 1024], P('gy', 'gx'), may hold values from 0.3 to 3
- ice_mask: int32 [512, 1024], P('gy', 'gx'), may hold values from 0 to 1
- land_mask: int32 [512, 1024], P('gy', 'gx'), may hold values from 0 to 1
Outputs:
- velocity_out: float32 [2, 512, 1024], P(None, 'gy', 'gx')
The draws below stay inside these ranges and needn't reach their ends.
All inputs are finite; a program needn't handle non-finite values.
Results may differ from the reference program's by a relative error of at most 0.0012.
Values sent between devices are 32-bit elements; how exact they have to be, the bound alone decides.
A program may use at most 64 MiB of HBM per device.

```python
import math
import jax
import jax.numpy as jnp
from jax import lax

CX = 128
CY = 128
PASSES = 2
NX = 1024
NY = 512


def rectangles(key, count):
    row_ids = lax.broadcasted_iota(jnp.int32, (NY, NX), 0)
    col_ids = lax.broadcasted_iota(jnp.int32, (NY, NX), 1)
    row_least = max(NY // 32, 1)
    row_most = max(NY // 8, row_least + 1)
    col_least = max(NX // 32, 1)
    col_most = max(NX // 8, col_least + 1)
    covered = jnp.zeros((NY, NX), jnp.int32)
    for rect_index in range(count):
        subkeys = jax.random.split(jax.random.fold_in(key, rect_index), 4)
        first_row = jax.random.randint(subkeys[0], (), 0, NY)
        row_span = jax.random.randint(subkeys[1], (), row_least, row_most)
        first_col = jax.random.randint(subkeys[2], (), 0, NX)
        col_span = jax.random.randint(subkeys[3], (), col_least, col_most)
        inside = (row_ids >= first_row) & (row_ids < first_row + row_span) & (col_ids >= first_col) & (col_ids < first_col + col_span)
        covered = jnp.maximum(covered, inside.astype(jnp.int32))
    return covered


def draw_ice_mask(key, part):
    holes = rectangles(jax.random.fold_in(key, 11), 8)
    return (1 - holes).astype(jnp.int32)


def draw_land_mask(key, part):
    return rectangles(jax.random.fold_in(key, 23), 8).astype(jnp.int32)


def draw_wind_stress(key, part):
    base_key = jax.random.fold_in(key, 37)
    return jnp.clip(jax.random.normal(base_key, (2, NY, NX), jnp.float32), -6.0, 6.0)


def levels(key, dims, cuts, smallest, largest):
    gain = 1.0
    for axis_at, parts in cuts:
        draws = jax.random.uniform(jax.random.fold_in(jax.random.fold_in(key, 6), axis_at), (parts,), jnp.float32, smallest / len(cuts), largest / len(cuts))
        gain = gain * jnp.repeat(jnp.exp(draws), dims[axis_at] // parts).reshape((-1,) + (1,) * (len(dims) - 1 - axis_at))
    return gain


def scatter_about(key, shape, scale, bound, cuts=(), dtype=jnp.bfloat16):
    result = scale * jax.random.normal(key, shape, jnp.float32)
    if cuts:
        result = result * levels(key, shape, cuts, -0.22, 0.18)
    return jnp.clip(result, -bound, bound).astype(dtype)


def setup_inputs(seed: int = 0) -> dict:
    streams_of = jax.random.split(jax.random.key(seed), 6)
    return {
        "velocity": scatter_about(streams_of[0], (2, NY, NX), 1.0, 6.0, ((1, 4), (2, 8)), jnp.float32),
        "wind_stress": draw_wind_stress(jax.random.fold_in(streams_of[5], 71), 0),
        "thickness": jnp.clip(jnp.exp(math.log(3.0) - 2.3025851 * jax.random.uniform(streams_of[2], (NY, NX), jnp.float32) ** levels(streams_of[2], (NY, NX), ((0, 4), (1, 8)), -0.2, 0.2)), 0.3, 3.0),
        "ice_mask": draw_ice_mask(jax.random.fold_in(streams_of[5], 71), 0),
        "land_mask": draw_land_mask(jax.random.fold_in(streams_of[5], 71), 0),
    }


CORIOLIS = 1.0
DELTA_MIN = 0.25
WIND_GAIN = 0.2

def shift_below(array, stride, fill_value):
    filler = jnp.full(array.shape[:-1] + (stride,), fill_value, jnp.float32)
    return jnp.concatenate([filler, array[..., :-stride]], axis=-1)

def shift_above(array, stride, fill_value):
    filler = jnp.full(array.shape[:-1] + (stride,), fill_value, jnp.float32)
    return jnp.concatenate([array[..., stride:], filler], axis=-1)

def reduce_lines(lower_band, middle, upper_band, right_side):
    line_total = right_side.shape[-1]
    stride = 1
    while stride < line_total:
        low_lower = shift_below(lower_band, stride, 0.0)
        low_mid = shift_below(middle, stride, 1.0)
        low_upper = shift_below(upper_band, stride, 0.0)
        low_right = shift_below(right_side, stride, 0.0)
        high_lower = shift_above(lower_band, stride, 0.0)
        high_mid = shift_above(middle, stride, 1.0)
        high_upper = shift_above(upper_band, stride, 0.0)
        high_right = shift_above(right_side, stride, 0.0)
        weight_low = -lower_band / low_mid
        weight_high = -upper_band / high_mid
        lower_band, middle, upper_band, right_side = (weight_low * low_lower, middle + weight_low * low_upper + weight_high * high_lower, weight_high * high_upper, right_side + weight_low * low_right + weight_high * high_right)
        stride *= 2
    return right_side / middle

def viscosity_of(u_rim, v_rim, thickness):
    strain_xx = 0.5 * (u_rim[1:-1, 2:] - u_rim[1:-1, :-2])
    strain_yy = 0.5 * (v_rim[2:, 1:-1] - v_rim[:-2, 1:-1])
    shear = 0.25 * (u_rim[2:, 1:-1] - u_rim[:-2, 1:-1] + (v_rim[1:-1, 2:] - v_rim[1:-1, :-2]))
    delta2 = 1.25 * (strain_xx * strain_xx + strain_yy * strain_yy) + shear * shear + 1.5 * strain_xx * strain_yy
    return thickness / (2.0 * jnp.sqrt(delta2 + DELTA_MIN * DELTA_MIN))

def edge_terms(visc_rim):
    centre = visc_rim[1:-1, 1:-1]
    east_edge = jnp.sqrt(centre * visc_rim[1:-1, 2:])
    west_edge = jnp.sqrt(centre * visc_rim[1:-1, :-2])
    north_edge = jnp.sqrt(centre * visc_rim[2:, 1:-1])
    south_edge = jnp.sqrt(centre * visc_rim[:-2, 1:-1])
    return (east_edge, west_edge, north_edge, south_edge)

def u_system(edges, live, ice_mass, weak, press, u_rim, v_speed, wind_x, p_rim):
    east_edge, west_edge, north_edge, south_edge = edges
    centre = ice_mass + east_edge + west_edge + weak * (north_edge + south_edge)
    right_side = ice_mass * u_rim[1:-1, 1:-1] + wind_x + CORIOLIS * ice_mass * v_speed + weak * (north_edge * u_rim[2:, 1:-1] + south_edge * u_rim[:-2, 1:-1]) - 0.5 * press * (p_rim[1:-1, 2:] - p_rim[1:-1, :-2])
    return (jnp.where(live, -west_edge, 0.0), jnp.where(live, centre, 1.0), jnp.where(live, -east_edge, 0.0), jnp.where(live, right_side, 0.0))

def v_system(edges, live, ice_mass, weak, press, v_rim, u_speed, wind_y, p_rim):
    east_edge, west_edge, north_edge, south_edge = edges
    centre = ice_mass + north_edge + south_edge + weak * (east_edge + west_edge)
    right_side = ice_mass * v_rim[1:-1, 1:-1] + wind_y - CORIOLIS * ice_mass * u_speed + weak * (east_edge * v_rim[1:-1, 2:] + west_edge * v_rim[1:-1, :-2]) - 0.5 * press * (p_rim[2:, 1:-1] - p_rim[:-2, 1:-1])
    return (jnp.where(live, -south_edge, 0.0), jnp.where(live, centre, 1.0), jnp.where(live, -north_edge, 0.0), jnp.where(live, right_side, 0.0))

def reference(velocity, wind_stress, thickness, ice_mask, land_mask):
    active = (ice_mask * (1 - land_mask)).astype(jnp.float32)
    live = active > 0.5
    cell_count = float(CX * CY)
    weak = 1.0 / (16.0 * cell_count)
    press = cell_count ** (-0.25)
    drive = WIND_GAIN * cell_count ** (-0.75)
    ice_mass = weak * thickness
    wind_x = drive * wind_stress[0]
    wind_y = drive * wind_stress[1]
    u_speed = velocity[0]
    v_speed = velocity[1]
    p_rim = jnp.pad(thickness, 1)
    for sweep in range(PASSES):
        u_rim = jnp.pad(u_speed, 1)
        v_rim = jnp.pad(v_speed, 1)
        viscosity = viscosity_of(u_rim, v_rim, thickness)
        edges = edge_terms(jnp.pad(viscosity, 1))
        system = u_system(edges, live, ice_mass, weak, press, u_rim, v_speed, wind_x, p_rim)
        u_speed = reduce_lines(*system)
        system = v_system(edges, live, ice_mass, weak, press, v_rim, u_speed, wind_y, p_rim)
        turned = [part.T for part in system]
        v_speed = reduce_lines(*turned).T
    return jnp.stack([u_speed, v_speed])
```

```python
import functools

import jax
import jax.numpy as jnp
from jax import lax
from jax.experimental import pallas as pl
from jax.experimental.pallas import tpu as pltpu
from jax.sharding import PartitionSpec as P

PASSES = 2
CORIOLIS = 1.0
DELTA_MIN = 0.25
WIND_GAIN = 0.2
MESH = pl.DeviceIdType.MESH

XM, XP, YM, YP = 0, 1, 2, 3
AXIS = ("gx", "gx", "gy", "gy")
STEP = (-1, 1, -1, 1)


def below(array, stride, fill):
    rows = array.shape[0]
    if stride % 8 == 0:
        filler = jnp.broadcast_to(jnp.float32(fill), (stride, array.shape[1]))
        return jnp.concatenate([filler, array[:-stride]], axis=0)
    row = lax.broadcasted_iota(jnp.int32, array.shape, 0)
    return jnp.where(row < stride, fill, pltpu.roll(array, stride, 0))


def above(array, stride, fill):
    rows = array.shape[0]
    if stride % 8 == 0:
        filler = jnp.broadcast_to(jnp.float32(fill), (stride, array.shape[1]))
        return jnp.concatenate([array[stride:], filler], axis=0)
    row = lax.broadcasted_iota(jnp.int32, array.shape, 0)
    return jnp.where(row >= rows - stride, fill, pltpu.roll(array, rows - stride, 0))


def reduce_matrix(low, excess, high):
    inv = 1.0 / (excess + low + high)
    first = inv
    p, q, f = low * inv, high * inv, excess * inv
    steps = []
    stride = 1
    while stride < low.shape[0]:
        p_next = p * below(p, stride, 1.0)
        q_next = q * above(q, stride, 1.0)
        f_next = f + p * below(f, stride, 0.0) + q * above(f, stride, 0.0)
        inv = 1.0 / (f_next + p_next + q_next)
        steps.append((stride, p, q, inv))
        p, q, f = p_next * inv, q_next * inv, f_next * inv
        stride *= 2
    return first, steps, p, q, f


def reduce_right(right, first, steps):
    g = right * first
    for stride, p, q, inv in steps:
        g = (g + p * below(g, stride, 0.0) + q * above(g, stride, 0.0)) * inv
    return g


def pack_ends(g, p, q, f):
    return jnp.concatenate(
        [g[:1], p[:1], q[:1], f[:1], g[-1:], p[-1:], q[-1:], f[-1:]], axis=0
    )


def left_step(rows, state):
    g0, p0, q0, f0, g1, p1, q1, f1 = rows
    a, b, c = state
    inv = 1.0 / (f0 + q0 + p0 * c)
    head_a = (g0 + p0 * a) * inv
    head_b = q0 * inv
    head_c = (f0 + p0 * c) * inv
    new = (
        g1 + p1 * (a + b * head_a),
        q1 + p1 * (b * head_b),
        f1 + p1 * (c + b * head_c),
    )
    return new, (head_a, head_b)


def right_step(rows, state):
    g0, p0, q0, f0, g1, p1, q1, f1 = rows
    new, _ = left_step((g1, q1, p1, f1, g0, q0, p0, f0), state)
    return new


def outer_values(block_of, me, count):
    mine = block_of(me)
    zero = jnp.zeros_like(mine[0])
    left = (zero, zero, zero + 1.0)
    right = (zero, zero, zero + 1.0)
    for j in range(count - 1):
        new, _ = left_step(block_of(j), left)
        left = tuple(jnp.where(j < me, n, o) for n, o in zip(new, left))
        k = count - 1 - j
        new = right_step(block_of(k), right)
        right = tuple(jnp.where(k > me, n, o) for n, o in zip(new, right))
    (a, b, c), (head_a, head_b) = left_step(mine, left)
    ra, rb, rc = right
    last = (a + b * ra) / (c + b * rc)
    after = ra + rb * last
    before = left[0] + left[1] * (head_a + head_b * after)
    return before, after


def kernel(
    sizes,
    velocity, wind, thickness_ref, ice, land,
    out,
    halo_out, halo_in, ends_x, ends_y,
    halo_send, halo_recv, x_send, x_recv, y_send, y_recv,
):
    me = {name: lax.axis_index(name) for name in ("gx", "gy")}
    barrier = pltpu.get_barrier_semaphore()
    total = 0
    for name in ("gx", "gy"):
        for k in range(1, sizes[name]):
            pl.semaphore_signal(
                barrier,
                device_id={name: lax.rem(me[name] + k, sizes[name])},
                device_id_type=MESH,
            )
            total += 1

    def has(direction):
        name = AXIS[direction]
        if STEP[direction] < 0:
            return me[name] > 0
        return me[name] < sizes[name] - 1

    def halo_copy(slot, direction):
        return pltpu.make_async_remote_copy(
            src_ref=halo_out.at[slot, direction],
            dst_ref=halo_in.at[slot, direction ^ 1],
            send_sem=halo_send.at[slot, direction],
            recv_sem=halo_recv.at[slot, direction ^ 1],
            device_id={AXIS[direction]: me[AXIS[direction]] + STEP[direction]},
            device_id_type=MESH,
        )

    def halo_start(slot, direction, rows):
        for n, row in enumerate(rows):
            halo_out[slot, direction, n : n + 1, :] = row

        @pl.when(has(direction))
        def _():
            halo_copy(slot, direction).start()

    def halo_wait(slot, direction, count):
        @pl.when(has(direction))
        def _():
            pltpu.make_async_remote_copy(
                src_ref=halo_out.at[slot, direction],
                dst_ref=halo_in.at[slot, direction],
                send_sem=halo_send.at[slot, direction],
                recv_sem=halo_recv.at[slot, direction],
                device_id={AXIS[direction]: me[AXIS[direction]] + STEP[direction]},
                device_id_type=MESH,
            ).wait()

        block = jnp.where(has(direction), halo_in[slot, direction], 0.0)
        return [block[n : n + 1] for n in range(count)]

    def ends_copy(name, buf, sweep, send, recv, k, source):
        return pltpu.make_async_remote_copy(
            src_ref=buf.at[sweep, source],
            dst_ref=buf.at[sweep, source],
            send_sem=send.at[sweep, k - 1],
            recv_sem=recv.at[sweep, k - 1],
            device_id={name: lax.rem(me[name] + k, sizes[name])},
            device_id_type=MESH,
        )

    def gather_start(name, buf, sweep, send, recv, block):
        buf[sweep, me[name]] = block
        for k in range(1, sizes[name]):
            ends_copy(name, buf, sweep, send, recv, k, me[name]).start()

    def gather_wait(name, buf, sweep, send, recv):
        count = sizes[name]
        for k in range(1, count):
            source = lax.rem(me[name] + count - k, count)
            ends_copy(name, buf, sweep, send, recv, k, source).wait_recv()

        def block_of(j):
            block = buf[sweep, j]
            return [block[n : n + 1] for n in range(8)]

        return outer_values(block_of, me[name], count)

    def gather_finish(name, buf, sweep, send, recv):
        for k in range(1, sizes[name]):
            ends_copy(name, buf, sweep, send, recv, k, me[name]).wait_send()

    cy, cx = thickness_ref.shape
    cell_count = float(cy * cx)
    weak = 1.0 / (16.0 * cell_count)
    press = cell_count ** (-0.25)
    drive = WIND_GAIN * cell_count ** (-0.75)

    u, v = velocity[0], velocity[1]
    thickness = thickness_ref[...]
    u_t, v_t, thickness_t = u.T, v.T, thickness.T

    pl.semaphore_wait(barrier, total)
    halo_start(0, XM, (u_t[:1], v_t[:1], thickness_t[:1]))
    halo_start(0, XP, (u_t[-1:], v_t[-1:], thickness_t[-1:]))
    halo_start(0, YM, (u[:1], v[:1], thickness[:1]))
    halo_start(0, YP, (u[-1:], v[-1:], thickness[-1:]))

    active = (ice[...] * (1 - land[...])).astype(jnp.float32)
    live = active > 0.5
    live_t = active.T > 0.5
    ice_mass = weak * thickness
    wind_x = drive * wind[0]
    wind_y = drive * wind[1]

    u_xm, v_xm, p_xm = halo_wait(0, XM, 3)
    u_xp, v_xp, p_xp = halo_wait(0, XP, 3)
    u_ym, v_ym, p_ym = halo_wait(0, YM, 3)
    u_yp, v_yp, p_yp = halo_wait(0, YP, 3)
    press_x = 0.5 * press * (above(thickness_t, 1, p_xp) - below(thickness_t, 1, p_xm))
    press_y = 0.5 * press * (above(thickness, 1, p_yp) - below(thickness, 1, p_ym))

    for sweep in range(PASSES):
        if sweep:
            (v_xm,) = halo_wait(2 * sweep, XM, 1)
            (v_xp,) = halo_wait(2 * sweep, XP, 1)
            (u_ym,) = halo_wait(2 * sweep, YM, 1)
            (u_yp,) = halo_wait(2 * sweep, YP, 1)
        v_east, v_west = above(v_t, 1, v_xp), below(v_t, 1, v_xm)
        u_north, u_south = above(u, 1, u_yp), below(u, 1, u_ym)
        strain_xx = (0.5 * (above(u_t, 1, u_xp) - below(u_t, 1, u_xm))).T
        strain_yy = 0.5 * (above(v, 1, v_yp) - below(v, 1, v_ym))
        shear = 0.25 * ((u_north - u_south) + (v_east - v_west).T)
        delta2 = (
            1.25 * (strain_xx * strain_xx + strain_yy * strain_yy)
            + shear * shear
            + 1.5 * strain_xx * strain_yy
        )
        visc = thickness / (2.0 * jnp.sqrt(delta2 + DELTA_MIN * DELTA_MIN))
        slot = 2 * sweep + 1
        halo_start(slot, YM, (visc[:1],))
        halo_start(slot, YP, (visc[-1:],))
        visc_t = visc.T
        halo_start(slot, XM, (visc_t[:1],))
        halo_start(slot, XP, (visc_t[-1:],))
        (visc_ym,) = halo_wait(slot, YM, 1)
        (visc_yp,) = halo_wait(slot, YP, 1)
        north = jnp.sqrt(visc * above(visc, 1, visc_yp))
        south = jnp.sqrt(visc * below(visc, 1, visc_ym))
        (visc_xm,) = halo_wait(slot, XM, 1)
        (visc_xp,) = halo_wait(slot, XP, 1)
        east = jnp.sqrt(visc_t * above(visc_t, 1, visc_xp))
        west = jnp.sqrt(visc_t * below(visc_t, 1, visc_xm))

        excess = (ice_mass + weak * (north + south)).T
        right = (
            ice_mass * u + wind_x + CORIOLIS * ice_mass * v
            + weak * (north * u_north + south * u_south)
        ).T - press_x
        first, steps, p, q, f = reduce_matrix(
            jnp.where(live_t, west, 0.0),
            jnp.where(live_t, excess, 1.0),
            jnp.where(live_t, east, 0.0),
        )
        g = reduce_right(jnp.where(live_t, right, 0.0), first, steps)
        gather_start("gx", ends_x, sweep, x_send, x_recv, pack_ends(g, p, q, f))

        excess = ice_mass + (weak * (east + west)).T
        first, steps, p_y, q_y, f_y = reduce_matrix(
            jnp.where(live, south, 0.0),
            jnp.where(live, excess, 1.0),
            jnp.where(live, north, 0.0),
        )
        right = (
            ice_mass * v + wind_y
            + (weak * (east * v_east + west * v_west)).T
            - press_y
        )

        u_xm, u_xp = gather_wait("gx", ends_x, sweep, x_send, x_recv)
        u_t = g + p * u_xm + q * u_xp
        u = u_t.T
        if sweep + 1 < PASSES:
            halo_start(2 * sweep + 2, YM, (u[:1],))
            halo_start(2 * sweep + 2, YP, (u[-1:],))
        right = right - CORIOLIS * ice_mass * u
        g = reduce_right(jnp.where(live, right, 0.0), first, steps)
        gather_start("gy", ends_y, sweep, y_send, y_recv, pack_ends(g, p_y, q_y, f_y))
        v_ym, v_yp = gather_wait("gy", ends_y, sweep, y_send, y_recv)
        v = g + p_y * v_ym + q_y * v_yp
        if sweep + 1 < PASSES:
            v_t = v.T
            halo_start(2 * sweep + 2, XM, (v_t[:1],))
            halo_start(2 * sweep + 2, XP, (v_t[-1:],))
    out[0] = u
    out[1] = v
    for sweep in range(PASSES):
        gather_finish("gx", ends_x, sweep, x_send, x_recv)
        gather_finish("gy", ends_y, sweep, y_send, y_recv)


def on_device(sizes, velocity, wind_stress, thickness, ice_mask, land_mask):
    cy, cx = thickness.shape
    wide = max(cx, cy)
    vmem = pl.BlockSpec(memory_space=pltpu.VMEM)
    nx, ny = sizes["gx"], sizes["gy"]
    slots = 2 * PASSES
    return pl.pallas_call(
        functools.partial(kernel, sizes),
        out_shape=jax.ShapeDtypeStruct(velocity.shape, jnp.float32),
        in_specs=[vmem] * 5,
        out_specs=vmem,
        scratch_shapes=[
            pltpu.VMEM((slots, 4, 8, wide), jnp.float32),
            pltpu.VMEM((slots, 4, 8, wide), jnp.float32),
            pltpu.VMEM((PASSES, nx, 8, cy), jnp.float32),
            pltpu.VMEM((PASSES, ny, 8, cx), jnp.float32),
            pltpu.SemaphoreType.DMA((slots, 4)),
            pltpu.SemaphoreType.DMA((slots, 4)),
            pltpu.SemaphoreType.DMA((PASSES, nx - 1)),
            pltpu.SemaphoreType.DMA((PASSES, nx - 1)),
            pltpu.SemaphoreType.DMA((PASSES, ny - 1)),
            pltpu.SemaphoreType.DMA((PASSES, ny - 1)),
        ],
        compiler_params=pltpu.CompilerParams(collective_id=0, has_side_effects=True),
        name="ice_relaxation",
    )(velocity, wind_stress, thickness, ice_mask, land_mask)


def solution(mesh):
    sizes = {name: int(mesh.shape[name]) for name in ("gx", "gy")}
    cells = P("gy", "gx")
    pairs = P(None, "gy", "gx")
    return jax.shard_map(
        functools.partial(on_device, sizes),
        mesh=mesh,
        in_specs=(pairs, pairs, cells, cells, cells),
        out_specs=pairs,
        check_vma=False,
    )
```

```python
import functools

import jax
import jax.numpy as jnp
from jax import lax
from jax.experimental import pallas as pl
from jax.experimental.pallas import tpu as pltpu
from jax.sharding import PartitionSpec as P

PASSES = 2
CORIOLIS = 1.0
DELTA_MIN = 0.25
WIND_GAIN = 0.2
MESH = pl.DeviceIdType.MESH

XM, XP, YM, YP = 0, 1, 2, 3
AXIS = ("gx", "gx", "gy", "gy")
STEP = (-1, 1, -1, 1)


def below(array, stride, fill):
    rows = array.shape[0]
    if stride % 8 == 0:
        filler = jnp.broadcast_to(jnp.float32(fill), (stride, array.shape[1]))
        return jnp.concatenate([filler, array[:-stride]], axis=0)
    row = lax.broadcasted_iota(jnp.int32, array.shape, 0)
    return jnp.where(row < stride, fill, pltpu.roll(array, stride, 0))


def above(array, stride, fill):
    rows = array.shape[0]
    if stride % 8 == 0:
        filler = jnp.broadcast_to(jnp.float32(fill), (stride, array.shape[1]))
        return jnp.concatenate([array[stride:], filler], axis=0)
    row = lax.broadcasted_iota(jnp.int32, array.shape, 0)
    return jnp.where(row >= rows - stride, fill, pltpu.roll(array, rows - stride, 0))


def reduce_matrix(low, excess, high):
    inv = 1.0 / (excess + low + high)
    first = inv
    p, q, f = low * inv, high * inv, excess * inv
    steps = []
    stride = 1
    while stride < low.shape[0]:
        p_next = p * below(p, stride, 1.0)
        q_next = q * above(q, stride, 1.0)
        f_next = f + p * below(f, stride, 0.0) + q * above(f, stride, 0.0)
        inv = 1.0 / (f_next + p_next + q_next)
        steps.append((stride, p, q, inv))
        p, q, f = p_next * inv, q_next * inv, f_next * inv
        stride *= 2
    return first, steps, p, q, f


def reduce_right(right, first, steps):
    g = right * first
    for stride, p, q, inv in steps:
        g = (g + p * below(g, stride, 0.0) + q * above(g, stride, 0.0)) * inv
    return g


def ends_matrix(p, q, f):
    return jnp.concatenate([p[:1], q[:1], f[:1], p[-1:], q[-1:], f[-1:]], axis=0)


def ends_right(g):
    return jnp.concatenate([g[:1], g[-1:]], axis=0)


def link(matrix, b, c):
    p0, q0, f0, p1, q1, f1 = matrix
    inv = 1.0 / (f0 + q0 + p0 * c)
    head_b = q0 * inv
    head_c = (f0 + p0 * c) * inv
    through = p1 * b * inv
    gains = (p1 + through * p0, through)
    return q1 + p1 * (b * head_b), f1 + p1 * (c + b * head_c), gains, (inv, head_b)


def chain_matrix(matrix_of, me, count):
    mine = matrix_of(me)
    zero = jnp.zeros_like(mine[0])
    lb, lc, rb, rc = zero, zero + 1.0, zero, zero + 1.0
    links = []
    for j in range(count - 1):
        nb, nc, gains, _ = link(matrix_of(j), lb, lc)
        take = j < me
        lb, lc = jnp.where(take, nb, lb), jnp.where(take, nc, lc)
        k = count - 1 - j
        p0, q0, f0, p1, q1, f1 = matrix_of(k)
        nb, nc, back, _ = link((q1, p1, f1, q0, p0, f0), rb, rc)
        take = k > me
        rb, rc = jnp.where(take, nb, rb), jnp.where(take, nc, rc)
        links.append((gains, back))
    b, c, gains, (inv, head_b) = link(mine, lb, lc)
    last_inv = 1.0 / (c + b * rc)
    return links, gains, mine[0] * inv, inv, head_b, lb, b, rb, last_inv


def chain_right(right_of, chain, me, count):
    links, gains, p0_inv, inv, head_b, left_b, b, rb, last_inv = chain
    mine = right_of(me)
    left = right = jnp.zeros_like(mine[0])
    for j, (ahead, back) in enumerate(links):
        g0, g1 = right_of(j)
        left = jnp.where(j < me, g1 + ahead[0] * left + ahead[1] * g0, left)
        k = count - 1 - j
        g0, g1 = right_of(k)
        right = jnp.where(k > me, g0 + back[0] * right + back[1] * g1, right)
    a = mine[1] + gains[0] * left + gains[1] * mine[0]
    last = (a + b * right) * last_inv
    after = right + rb * last
    before = left + left_b * (mine[0] * inv + p0_inv * left + head_b * after)
    return before, after


def lane_below(row, corner):
    lane = lax.broadcasted_iota(jnp.int32, row.shape, 1)
    return jnp.where(lane == 0, corner, pltpu.roll(row, 1, 1))


def lane_above(row, corner):
    lane = lax.broadcasted_iota(jnp.int32, row.shape, 1)
    return jnp.where(
        lane == row.shape[1] - 1, corner, pltpu.roll(row, row.shape[1] - 1, 1)
    )


def viscosity_of(strain_xx, strain_yy, shear, thickness):
    delta2 = (
        1.25 * (strain_xx * strain_xx + strain_yy * strain_yy)
        + shear * shear
        + 1.5 * strain_xx * strain_yy
    )
    return thickness / (2.0 * jnp.sqrt(delta2 + DELTA_MIN * DELTA_MIN))


def kernel(
    sizes,
    velocity_hbm, wind_hbm, thickness_hbm, ice_hbm, land_hbm,
    out,
    velocity, wind, thickness_ref, ice, land, in_sem,
    halo_out, halo_in, diag_out, diag_in,
    x_matrix, x_right, y_matrix, y_right, y_steps, y_rest,
    halo_send, halo_recv, diag_send, diag_recv,
    xm_send, xm_recv, xr_send, xr_recv, ym_send, ym_recv, yr_send, yr_recv,
):
    me = {name: lax.axis_index(name) for name in ("gx", "gy")}
    loads = [
        pltpu.make_async_copy(src, dst, in_sem.at[n])
        for n, (src, dst) in enumerate(
            (
                (velocity_hbm, velocity), (thickness_hbm, thickness_ref),
                (wind_hbm, wind), (ice_hbm, ice), (land_hbm, land),
            )
        )
    ]
    for load in loads:
        load.start()

    def has(direction):
        name = AXIS[direction]
        if STEP[direction] < 0:
            return me[name] > 0
        return me[name] < sizes[name] - 1

    corners = [(x, y) for x in (XM, XP) for y in (YM, YP)]

    def corner_id(x, y):
        return {"gx": me["gx"] + STEP[x], "gy": me["gy"] + STEP[y]}

    def has_corner(x, y):
        return jnp.logical_and(has(x), has(y))

    barrier = pltpu.get_barrier_semaphore()
    total = 0
    for name in ("gx", "gy"):
        for k in range(1, sizes[name]):
            pl.semaphore_signal(
                barrier,
                device_id={name: lax.rem(me[name] + k, sizes[name])},
                device_id_type=MESH,
            )
            total += 1
    for x, y in corners:
        total = total + jnp.where(has_corner(x, y), 1, 0)

        @pl.when(has_corner(x, y))
        def _():
            pl.semaphore_signal(
                barrier, device_id=corner_id(x, y), device_id_type=MESH
            )

    def halo_copy(slot, direction, landing):
        return pltpu.make_async_remote_copy(
            src_ref=halo_out.at[slot, direction],
            dst_ref=halo_in.at[slot, landing],
            send_sem=halo_send.at[slot, direction],
            recv_sem=halo_recv.at[slot, landing],
            device_id={AXIS[direction]: me[AXIS[direction]] + STEP[direction]},
            device_id_type=MESH,
        )

    def halo_fill(slot, direction, rows):
        for n, row in enumerate(rows):
            halo_out[slot, direction, n : n + 1, : row.shape[1]] = row

    def halo_start(slot, direction):
        @pl.when(has(direction))
        def _():
            halo_copy(slot, direction, direction ^ 1).start()

    def halo_wait(slot, direction, count):
        @pl.when(has(direction))
        def _():
            halo_copy(slot, direction, direction).wait()

        wide = cy if AXIS[direction] == "gx" else cx
        block = jnp.where(has(direction), halo_in[slot, direction, :, :wide], 0.0)
        return [block[n : n + 1] for n in range(count)]

    def diag_copy(n, landing):
        return pltpu.make_async_remote_copy(
            src_ref=diag_out.at[n],
            dst_ref=diag_in.at[landing],
            send_sem=diag_send.at[n],
            recv_sem=diag_recv.at[landing],
            device_id=corner_id(*corners[n]),
            device_id_type=MESH,
        )

    def ends_copy(name, ends, sweep, k, source):
        buf, send, recv = ends
        return pltpu.make_async_remote_copy(
            src_ref=buf.at[sweep, source],
            dst_ref=buf.at[sweep, source],
            send_sem=send.at[sweep, k - 1],
            recv_sem=recv.at[sweep, k - 1],
            device_id={name: lax.rem(me[name] + k, sizes[name])},
            device_id_type=MESH,
        )

    def gather_start(name, ends, sweep, block):
        ends[0][sweep, me[name]] = block
        for k in range(1, sizes[name]):
            ends_copy(name, ends, sweep, k, me[name]).start()

    def gather_wait(name, ends, sweep):
        count = sizes[name]
        for k in range(1, count):
            source = lax.rem(me[name] + count - k, count)
            ends_copy(name, ends, sweep, k, source).wait_recv()

        def block_of(j):
            block = ends[0][sweep, j]
            return [block[n : n + 1] for n in range(block.shape[0])]

        return block_of

    def outer_values(name, matrix, right, sweep):
        chain = chain_matrix(gather_wait(name, matrix, sweep), me[name], sizes[name])
        return chain_right(
            gather_wait(name, right, sweep), chain, me[name], sizes[name]
        )

    gathers = (
        ("gx", (x_matrix, xm_send, xm_recv)),
        ("gx", (x_right, xr_send, xr_recv)),
        ("gy", (y_matrix, ym_send, ym_recv)),
        ("gy", (y_right, yr_send, yr_recv)),
    )
    x_ends = (gathers[0][1], gathers[1][1])
    y_ends = (gathers[2][1], gathers[3][1])

    cy, cx = thickness_ref.shape
    cell_count = float(cy * cx)
    weak = 1.0 / (16.0 * cell_count)
    press = cell_count ** (-0.25)
    drive = WIND_GAIN * cell_count ** (-0.75)

    loads[0].wait()
    loads[1].wait()
    u, v = velocity[0], velocity[1]
    thickness = thickness_ref[...]
    u_t, v_t, thickness_t = u.T, v.T, thickness.T
    halo_fill(0, YM, (u[:1], v[:1], u[1:2], v[1:2], thickness[:1]))
    halo_fill(0, YP, (u[-1:], v[-1:], u[-2:-1], v[-2:-1], thickness[-1:]))
    for n, (x, y) in enumerate(corners):
        row = slice(0, 1) if y == YM else slice(cy - 1, cy)
        lane = slice(0, 1) if x == XM else slice(cx - 1, cx)
        for m, field in enumerate((u, v)):
            diag_out[n, m : m + 1, :] = jnp.broadcast_to(
                field[row, lane], (1, diag_out.shape[2])
            )
    halo_fill(0, XM, (u_t[:1], v_t[:1], u_t[1:2], v_t[1:2], thickness_t[:1]))
    halo_fill(0, XP, (u_t[-1:], v_t[-1:], u_t[-2:-1], v_t[-2:-1], thickness_t[-1:]))
    pl.semaphore_wait(barrier, total)
    for n in range(4):

        @pl.when(has_corner(*corners[n]))
        def _():
            diag_copy(n, 3 - n).start()

    for direction in (YM, YP, XM, XP):
        halo_start(0, direction)

    for load in loads[2:]:
        load.wait()
    active = (ice[...] * (1 - land[...])).astype(jnp.float32)
    live = active > 0.5
    live_t = active.T > 0.5
    ice_mass = weak * thickness
    wind_x = drive * wind[0]
    wind_y = drive * wind[1]

    for sweep in range(PASSES):
        if sweep == 0:
            u_xm, v_xm, u_xm2, v_xm2, p_xm = halo_wait(0, XM, 5)
            u_xp, v_xp, u_xp2, v_xp2, p_xp = halo_wait(0, XP, 5)
            u_ym, v_ym, u_ym2, v_ym2, p_ym = halo_wait(0, YM, 5)
            u_yp, v_yp, u_yp2, v_yp2, p_yp = halo_wait(0, YP, 5)
            corner = []
            for n in range(4):

                @pl.when(has_corner(*corners[n]))
                def _():
                    diag_copy(n, n).wait()

                block = jnp.where(has_corner(*corners[n]), diag_in[n], 0.0)
                corner.append([block[:1], block[1:2]])
            mm, mp, pm, pp = corner
            press_x = 0.5 * press * (
                above(thickness_t, 1, p_xp) - below(thickness_t, 1, p_xm)
            )
            press_y = 0.5 * press * (
                above(thickness, 1, p_yp) - below(thickness, 1, p_ym)
            )
        else:
            late = 2 * sweep
            u_xm, v_xm, u_xm2, v_xm2, *low = halo_wait(late, XM, 8)
            u_xp, v_xp, u_xp2, v_xp2, *high = halo_wait(late, XP, 8)
            mm, mp, pm, pp = low[:2], low[2:], high[:2], high[2:]
            (v_ym2,) = halo_wait(late, YM, 1)
            (v_yp2,) = halo_wait(late, YP, 1)

        v_east, v_west = above(v_t, 1, v_xp), below(v_t, 1, v_xm)
        u_north, u_south = above(u, 1, u_yp), below(u, 1, u_ym)
        strain_xx = (0.5 * (above(u_t, 1, u_xp) - below(u_t, 1, u_xm))).T
        strain_yy = 0.5 * (above(v, 1, v_yp) - below(v, 1, v_ym))
        shear = 0.25 * ((u_north - u_south) + (v_east - v_west).T)
        visc = viscosity_of(strain_xx, strain_yy, shear, thickness)

        def rim(near, minus1, minus2, plus1, plus2, m_lo, m_hi, p_lo, p_hi):
            across = jnp.concatenate([near[:1] - minus2, plus2 - near[-1:]], axis=0)
            n = minus1.shape[1]
            along = jnp.concatenate(
                [
                    lane_above(minus1, m_hi[:, :n]) - lane_below(minus1, m_lo[:, :n]),
                    lane_above(plus1, p_hi[:, :n]) - lane_below(plus1, p_lo[:, :n]),
                ],
                axis=0,
            )
            return across, along

        u_across, u_along = rim(
            u_t, u_xm, u_xm2, u_xp, u_xp2, mm[0], mp[0], pm[0], pp[0]
        )
        v_across, v_along = rim(
            v_t, v_xm, v_xm2, v_xp, v_xp2, mm[1], mp[1], pm[1], pp[1]
        )
        visc_x = viscosity_of(
            0.5 * u_across, 0.5 * v_along, 0.25 * (u_along + v_across),
            jnp.concatenate([p_xm, p_xp], axis=0),
        )
        u_across, u_along = rim(
            u, u_ym, u_ym2, u_yp, u_yp2, mm[0], pm[0], mp[0], pp[0]
        )
        v_across, v_along = rim(
            v, v_ym, v_ym2, v_yp, v_yp2, mm[1], pm[1], mp[1], pp[1]
        )
        visc_y = viscosity_of(
            0.5 * u_along, 0.5 * v_across, 0.25 * (u_across + v_along),
            jnp.concatenate([p_ym, p_yp], axis=0),
        )

        visc_t = visc.T
        north = jnp.sqrt(visc * above(visc, 1, visc_y[1:]))
        south = jnp.sqrt(visc * below(visc, 1, visc_y[:1]))
        east = jnp.sqrt(visc_t * above(visc_t, 1, visc_x[1:]))
        west = jnp.sqrt(visc_t * below(visc_t, 1, visc_x[:1]))

        excess = (ice_mass + weak * (north + south)).T
        right = (
            ice_mass * u + wind_x + CORIOLIS * ice_mass * v
            + weak * (north * u_north + south * u_south)
        ).T - press_x
        first, steps, p, q, f = reduce_matrix(
            jnp.where(live_t, west, 0.0),
            jnp.where(live_t, excess, 1.0),
            jnp.where(live_t, east, 0.0),
        )
        gather_start("gx", x_ends[0], sweep, ends_matrix(p, q, f))
        g = reduce_right(jnp.where(live_t, right, 0.0), first, steps)
        gather_start("gx", x_ends[1], sweep, ends_right(g))

        @pl.when(me["gx"] >= 0)
        def _():
            excess = ice_mass + (weak * (east + west)).T
            first, steps, p_y, q_y, f_y = reduce_matrix(
                jnp.where(live, south, 0.0),
                jnp.where(live, excess, 1.0),
                jnp.where(live, north, 0.0),
            )
            gather_start("gy", y_ends[0], sweep, ends_matrix(p_y, q_y, f_y))
            for n, (_, p_n, q_n, inv) in enumerate(steps):
                y_steps[n, 0], y_steps[n, 1], y_steps[n, 2] = p_n, q_n, inv
            right = (
                ice_mass * v + wind_y
                + (weak * (east * v_east + west * v_west)).T
                - press_y
            )
            y_rest[0], y_rest[1], y_rest[2], y_rest[3] = first, p_y, q_y, right

        u_xm, u_xp = outer_values("gx", *x_ends, sweep)
        u_t = g + p * u_xm + q * u_xp
        u = u_t.T
        if sweep + 1 < PASSES:
            early = 2 * sweep + 1
            halo_fill(early, YM, (u[:1], u[1:2]))
            halo_fill(early, YP, (u[-1:], u[-2:-1]))
            halo_start(early, YM)
            halo_start(early, YP)
        else:
            out[0] = u
        y_strides = [
            (2**n, y_steps[n, 0], y_steps[n, 1], y_steps[n, 2])
            for n in range(y_steps.shape[0])
        ]
        right = y_rest[3] - CORIOLIS * ice_mass * u
        g = reduce_right(jnp.where(live, right, 0.0), y_rest[0], y_strides)
        gather_start("gy", y_ends[1], sweep, ends_right(g))
        v_ym, v_yp = outer_values("gy", *y_ends, sweep)
        v = g + y_rest[1] * v_ym + y_rest[2] * v_yp
        if sweep + 1 < PASSES:
            late = early + 1
            halo_fill(late, YM, (v[1:2],))
            halo_fill(late, YP, (v[-2:-1],))
            halo_start(late, YM)
            halo_start(late, YP)
            u_ym, u_ym2 = halo_wait(early, YM, 2)
            u_yp, u_yp2 = halo_wait(early, YP, 2)
            v_t = v.T
            for direction, near, next_, lane in ((XM, 0, 1, 0), (XP, cx - 1, cx - 2, cx - 1)):
                rows = [
                    u_t[near : near + 1], v_t[near : near + 1],
                    u_t[next_ : next_ + 1], v_t[next_ : next_ + 1],
                ] + [
                    jnp.broadcast_to(row[:, lane : lane + 1], (1, halo_out.shape[3]))
                    for row in (u_ym, v_ym, u_yp, v_yp)
                ]
                halo_fill(late, direction, rows)
                halo_start(late, direction)
    out[1] = v
    for sweep in range(PASSES):
        for name, ends in gathers:
            for k in range(1, sizes[name]):
                ends_copy(name, ends, sweep, k, me[name]).wait_send()


def on_device(sizes, velocity, wind_stress, thickness, ice_mask, land_mask):
    cy, cx = thickness.shape
    wide = max(cx, cy)
    nx, ny = sizes["gx"], sizes["gy"]
    slots = 2 * PASSES - 1
    dma = pltpu.SemaphoreType.DMA
    strides = (cy - 1).bit_length()
    f32 = jnp.float32
    args = (velocity, wind_stress, thickness, ice_mask, land_mask)
    return pl.pallas_call(
        functools.partial(kernel, sizes),
        out_shape=jax.ShapeDtypeStruct(velocity.shape, f32),
        in_specs=[pl.BlockSpec(memory_space=pl.ANY)] * 5,
        out_specs=pl.BlockSpec(memory_space=pltpu.VMEM),
        scratch_shapes=[pltpu.VMEM(arg.shape, arg.dtype) for arg in args]
        + [
            dma((5,)),
            pltpu.VMEM((slots, 4, 8, wide), f32),
            pltpu.VMEM((slots, 4, 8, wide), f32),
            pltpu.VMEM((4, 2, wide), f32),
            pltpu.VMEM((4, 2, wide), f32),
            pltpu.VMEM((PASSES, nx, 6, cy), f32),
            pltpu.VMEM((PASSES, nx, 2, cy), f32),
            pltpu.VMEM((PASSES, ny, 6, cx), f32),
            pltpu.VMEM((PASSES, ny, 2, cx), f32),
            pltpu.VMEM((strides, 3, cy, cx), f32),
            pltpu.VMEM((4, cy, cx), f32),
            dma((slots, 4)), dma((slots, 4)), dma((4,)), dma((4,)),
        ]
        + [dma((PASSES, nx - 1))] * 4
        + [dma((PASSES, ny - 1))] * 4,
        compiler_params=pltpu.CompilerParams(collective_id=0, has_side_effects=True),
        name="ice_relaxation",
    )(*args)


def solution(mesh):
    sizes = {name: int(mesh.shape[name]) for name in ("gx", "gy")}
    cells = P("gy", "gx")
    pairs = P(None, "gy", "gx")
    return jax.shard_map(
        functools.partial(on_device, sizes),
        mesh=mesh,
        in_specs=(pairs, pairs, cells, cells, cells),
        out_specs=pairs,
        check_vma=False,
    )
```

```python
import functools

import jax
import jax.numpy as jnp
from jax import lax
from jax.experimental import pallas as pl
from jax.experimental.pallas import tpu as pltpu
from jax.sharding import PartitionSpec as P

PASSES = 2
CORIOLIS = 1.0
DELTA_MIN = 0.25
WIND_GAIN = 0.2
MESH = pl.DeviceIdType.MESH

XM, XP, YM, YP = 0, 1, 2, 3
AXIS = ("gx", "gx", "gy", "gy")
STEP = (-1, 1, -1, 1)


def below(array, stride, fill):
    rows = array.shape[0]
    if stride % 8 == 0:
        filler = jnp.broadcast_to(jnp.float32(fill), (stride, array.shape[1]))
        return jnp.concatenate([filler, array[:-stride]], axis=0)
    row = lax.broadcasted_iota(jnp.int32, array.shape, 0)
    return jnp.where(row < stride, fill, pltpu.roll(array, stride, 0))


def above(array, stride, fill):
    rows = array.shape[0]
    if stride % 8 == 0:
        filler = jnp.broadcast_to(jnp.float32(fill), (stride, array.shape[1]))
        return jnp.concatenate([array[stride:], filler], axis=0)
    row = lax.broadcasted_iota(jnp.int32, array.shape, 0)
    return jnp.where(row >= rows - stride, fill, pltpu.roll(array, rows - stride, 0))


def reduce_matrix(low, excess, high):
    inv = 1.0 / (excess + low + high)
    first = inv
    p, q, f = low * inv, high * inv, excess * inv
    steps = []
    stride = 1
    while stride < low.shape[0]:
        p_next = p * below(p, stride, 1.0)
        q_next = q * above(q, stride, 1.0)
        f_next = f + p * below(f, stride, 0.0) + q * above(f, stride, 0.0)
        inv = 1.0 / (f_next + p_next + q_next)
        steps.append((stride, p, q, inv))
        p, q, f = p_next * inv, q_next * inv, f_next * inv
        stride *= 2
    return first, steps, p, q, f


def reduce_right(right, first, steps):
    g = right * first
    for stride, p, q, inv in steps:
        g = (g + p * below(g, stride, 0.0) + q * above(g, stride, 0.0)) * inv
    return g


def ends_matrix(p, q, f):
    return jnp.concatenate([p[:1], q[:1], f[:1], p[-1:], q[-1:], f[-1:]], axis=0)


def ends_right(g):
    return jnp.concatenate([g[:1], g[-1:]], axis=0)


def link(matrix, b, c):
    p0, q0, f0, p1, q1, f1 = matrix
    inv = 1.0 / (f0 + q0 + p0 * c)
    head_b = q0 * inv
    head_c = (f0 + p0 * c) * inv
    through = p1 * b * inv
    gains = (p1 + through * p0, through)
    return q1 + p1 * (b * head_b), f1 + p1 * (c + b * head_c), gains, (inv, head_b)


def chain_matrix(matrix_of, me, count):
    mine = matrix_of(me)
    zero = jnp.zeros_like(mine[0])
    lb, lc, rb, rc = zero, zero + 1.0, zero, zero + 1.0
    links = []
    for j in range(count - 1):
        nb, nc, gains, _ = link(matrix_of(j), lb, lc)
        take = j < me
        lb, lc = jnp.where(take, nb, lb), jnp.where(take, nc, lc)
        k = count - 1 - j
        p0, q0, f0, p1, q1, f1 = matrix_of(k)
        nb, nc, back, _ = link((q1, p1, f1, q0, p0, f0), rb, rc)
        take = k > me
        rb, rc = jnp.where(take, nb, rb), jnp.where(take, nc, rc)
        links.append((gains, back))
    b, c, gains, (inv, head_b) = link(mine, lb, lc)
    last_inv = 1.0 / (c + b * rc)
    return links, gains, mine[0] * inv, inv, head_b, lb, b, rb, last_inv


def chain_right(right_of, chain, me, count):
    links, gains, p0_inv, inv, head_b, left_b, b, rb, last_inv = chain
    mine = right_of(me)
    left = right = jnp.zeros_like(mine[0])
    for j, (ahead, back) in enumerate(links):
        g0, g1 = right_of(j)
        left = jnp.where(j < me, g1 + ahead[0] * left + ahead[1] * g0, left)
        k = count - 1 - j
        g0, g1 = right_of(k)
        right = jnp.where(k > me, g0 + back[0] * right + back[1] * g1, right)
    a = mine[1] + gains[0] * left + gains[1] * mine[0]
    last = (a + b * right) * last_inv
    after = right + rb * last
    before = left + left_b * (mine[0] * inv + p0_inv * left + head_b * after)
    return before, after


def lane_below(row, corner):
    lane = lax.broadcasted_iota(jnp.int32, row.shape, 1)
    return jnp.where(lane == 0, corner, pltpu.roll(row, 1, 1))


def lane_above(row, corner):
    lane = lax.broadcasted_iota(jnp.int32, row.shape, 1)
    return jnp.where(
        lane == row.shape[1] - 1, corner, pltpu.roll(row, row.shape[1] - 1, 1)
    )


def viscosity_of(strain_xx, strain_yy, shear, thickness):
    delta2 = (
        1.25 * (strain_xx * strain_xx + strain_yy * strain_yy)
        + shear * shear
        + 1.5 * strain_xx * strain_yy
    )
    return thickness / (2.0 * jnp.sqrt(delta2 + DELTA_MIN * DELTA_MIN))


def kernel(
    sizes,
    velocity_hbm, wind_hbm, thickness_hbm, ice_hbm, land_hbm,
    out,
    velocity, wind, thickness_ref, ice, land, in_sem,
    halo_out, halo_in, diag_out, diag_in,
    x_matrix, x_right, y_matrix, y_right, y_steps, y_rest,
    halo_send, halo_recv, diag_send, diag_recv,
    xm_send, xm_recv, xr_send, xr_recv, ym_send, ym_recv, yr_send, yr_recv,
):
    me = {name: lax.axis_index(name) for name in ("gx", "gy")}
    loads = [
        pltpu.make_async_copy(src, dst, in_sem.at[n])
        for n, (src, dst) in enumerate(
            (
                (velocity_hbm, velocity), (thickness_hbm, thickness_ref),
                (wind_hbm, wind), (ice_hbm, ice), (land_hbm, land),
            )
        )
    ]
    for load in loads:
        load.start()

    def has(direction):
        name = AXIS[direction]
        if STEP[direction] < 0:
            return me[name] > 0
        return me[name] < sizes[name] - 1

    corners = [(x, y) for x in (XM, XP) for y in (YM, YP)]

    def corner_id(x, y):
        return {"gx": me["gx"] + STEP[x], "gy": me["gy"] + STEP[y]}

    def has_corner(x, y):
        return jnp.logical_and(has(x), has(y))

    barrier = pltpu.get_barrier_semaphore()
    total = 0
    for name in ("gx", "gy"):
        for k in range(1, sizes[name]):
            pl.semaphore_signal(
                barrier,
                device_id={name: lax.rem(me[name] + k, sizes[name])},
                device_id_type=MESH,
            )
            total += 1
    for x, y in corners:
        total = total + jnp.where(has_corner(x, y), 1, 0)

        @pl.when(has_corner(x, y))
        def _():
            pl.semaphore_signal(
                barrier, device_id=corner_id(x, y), device_id_type=MESH
            )

    def halo_copy(slot, direction, landing):
        return pltpu.make_async_remote_copy(
            src_ref=halo_out.at[slot, direction],
            dst_ref=halo_in.at[slot, landing],
            send_sem=halo_send.at[slot, direction],
            recv_sem=halo_recv.at[slot, landing],
            device_id={AXIS[direction]: me[AXIS[direction]] + STEP[direction]},
            device_id_type=MESH,
        )

    def halo_fill(slot, direction, rows):
        for n, row in enumerate(rows):
            halo_out[slot, direction, n : n + 1, : row.shape[1]] = row

    def halo_start(slot, direction):
        @pl.when(has(direction))
        def _():
            halo_copy(slot, direction, direction ^ 1).start()

    def halo_wait(slot, direction, count):
        @pl.when(has(direction))
        def _():
            halo_copy(slot, direction, direction).wait()

        wide = cy if AXIS[direction] == "gx" else cx
        block = jnp.where(has(direction), halo_in[slot, direction, :, :wide], 0.0)
        return [block[n : n + 1] for n in range(count)]

    def diag_copy(n, landing):
        return pltpu.make_async_remote_copy(
            src_ref=diag_out.at[n],
            dst_ref=diag_in.at[landing],
            send_sem=diag_send.at[n],
            recv_sem=diag_recv.at[landing],
            device_id=corner_id(*corners[n]),
            device_id_type=MESH,
        )

    def ends_copy(name, ends, sweep, k, source):
        buf, send, recv = ends
        return pltpu.make_async_remote_copy(
            src_ref=buf.at[sweep, source],
            dst_ref=buf.at[sweep, source],
            send_sem=send.at[sweep, k - 1],
            recv_sem=recv.at[sweep, k - 1],
            device_id={name: lax.rem(me[name] + k, sizes[name])},
            device_id_type=MESH,
        )

    def gather_start(name, ends, sweep, block):
        ends[0][sweep, me[name]] = block
        for k in range(1, sizes[name]):
            ends_copy(name, ends, sweep, k, me[name]).start()

    def gather_wait(name, ends, sweep):
        count = sizes[name]
        for k in range(1, count):
            source = lax.rem(me[name] + count - k, count)
            ends_copy(name, ends, sweep, k, source).wait_recv()

        def block_of(j):
            block = ends[0][sweep, j]
            return [block[n : n + 1] for n in range(block.shape[0])]

        return block_of

    def outer_values(name, matrix, right, sweep):
        chain = chain_matrix(gather_wait(name, matrix, sweep), me[name], sizes[name])
        return chain_right(
            gather_wait(name, right, sweep), chain, me[name], sizes[name]
        )

    gathers = (
        ("gx", (x_matrix, xm_send, xm_recv)),
        ("gx", (x_right, xr_send, xr_recv)),
        ("gy", (y_matrix, ym_send, ym_recv)),
        ("gy", (y_right, yr_send, yr_recv)),
    )
    x_ends = (gathers[0][1], gathers[1][1])
    y_ends = (gathers[2][1], gathers[3][1])

    cy, cx = thickness_ref.shape
    cell_count = float(cy * cx)
    weak = 1.0 / (16.0 * cell_count)
    press = cell_count ** (-0.25)
    drive = WIND_GAIN * cell_count ** (-0.75)

    loads[0].wait()
    loads[1].wait()
    u, v = velocity[0], velocity[1]
    thickness = thickness_ref[...]
    u_t, v_t, thickness_t = u.T, v.T, thickness.T
    halo_fill(0, YM, (u[:1], v[:1], u[1:2], v[1:2], thickness[:1]))
    halo_fill(0, YP, (u[-1:], v[-1:], u[-2:-1], v[-2:-1], thickness[-1:]))
    for n, (x, y) in enumerate(corners):
        row = slice(0, 1) if y == YM else slice(cy - 1, cy)
        lane = slice(0, 1) if x == XM else slice(cx - 1, cx)
        for m, field in enumerate((u, v)):
            diag_out[n, m : m + 1, :] = jnp.broadcast_to(
                field[row, lane], (1, diag_out.shape[2])
            )
    halo_fill(0, XM, (u_t[:1], v_t[:1], u_t[1:2], v_t[1:2], thickness_t[:1]))
    halo_fill(0, XP, (u_t[-1:], v_t[-1:], u_t[-2:-1], v_t[-2:-1], thickness_t[-1:]))
    pl.semaphore_wait(barrier, total)
    for n in range(4):

        @pl.when(has_corner(*corners[n]))
        def _():
            diag_copy(n, 3 - n).start()

    for direction in (YM, YP, XM, XP):
        halo_start(0, direction)

    for load in loads[2:]:
        load.wait()
    active = (ice[...] * (1 - land[...])).astype(jnp.float32)
    live = active > 0.5
    live_t = active.T > 0.5
    ice_mass = weak * thickness
    wind_x = drive * wind[0]
    wind_y = drive * wind[1]

    for sweep in range(PASSES):
        if sweep == 0:
            u_xm, v_xm, u_xm2, v_xm2, p_xm = halo_wait(0, XM, 5)
            u_xp, v_xp, u_xp2, v_xp2, p_xp = halo_wait(0, XP, 5)
            u_ym, v_ym, u_ym2, v_ym2, p_ym = halo_wait(0, YM, 5)
            u_yp, v_yp, u_yp2, v_yp2, p_yp = halo_wait(0, YP, 5)
            corner = []
            for n in range(4):

                @pl.when(has_corner(*corners[n]))
                def _():
                    diag_copy(n, n).wait()

                block = jnp.where(has_corner(*corners[n]), diag_in[n], 0.0)
                corner.append([block[:1], block[1:2]])
            mm, mp, pm, pp = corner
            press_x = 0.5 * press * (
                above(thickness_t, 1, p_xp) - below(thickness_t, 1, p_xm)
            )
            press_y = 0.5 * press * (
                above(thickness, 1, p_yp) - below(thickness, 1, p_ym)
            )
        else:
            late = 2 * sweep
            u_xm, v_xm, u_xm2, v_xm2, *low = halo_wait(late, XM, 8)
            u_xp, v_xp, u_xp2, v_xp2, *high = halo_wait(late, XP, 8)
            mm, mp, pm, pp = low[:2], low[2:], high[:2], high[2:]
            (v_ym2,) = halo_wait(late, YM, 1)
            (v_yp2,) = halo_wait(late, YP, 1)

        v_east, v_west = above(v_t, 1, v_xp), below(v_t, 1, v_xm)
        u_north, u_south = above(u, 1, u_yp), below(u, 1, u_ym)
        strain_xx = (0.5 * (above(u_t, 1, u_xp) - below(u_t, 1, u_xm))).T
        strain_yy = 0.5 * (above(v, 1, v_yp) - below(v, 1, v_ym))
        shear = 0.25 * ((u_north - u_south) + (v_east - v_west).T)
        visc = viscosity_of(strain_xx, strain_yy, shear, thickness)

        def rim(near, minus1, minus2, plus1, plus2, m_lo, m_hi, p_lo, p_hi):
            across = jnp.concatenate([near[:1] - minus2, plus2 - near[-1:]], axis=0)
            n = minus1.shape[1]
            along = jnp.concatenate(
                [
                    lane_above(minus1, m_hi[:, :n]) - lane_below(minus1, m_lo[:, :n]),
                    lane_above(plus1, p_hi[:, :n]) - lane_below(plus1, p_lo[:, :n]),
                ],
                axis=0,
            )
            return across, along

        u_across, u_along = rim(
            u_t, u_xm, u_xm2, u_xp, u_xp2, mm[0], mp[0], pm[0], pp[0]
        )
        v_across, v_along = rim(
            v_t, v_xm, v_xm2, v_xp, v_xp2, mm[1], mp[1], pm[1], pp[1]
        )
        visc_x = viscosity_of(
            0.5 * u_across, 0.5 * v_along, 0.25 * (u_along + v_across),
            jnp.concatenate([p_xm, p_xp], axis=0),
        )
        u_across, u_along = rim(
            u, u_ym, u_ym2, u_yp, u_yp2, mm[0], pm[0], mp[0], pp[0]
        )
        v_across, v_along = rim(
            v, v_ym, v_ym2, v_yp, v_yp2, mm[1], pm[1], mp[1], pp[1]
        )
        visc_y = viscosity_of(
            0.5 * u_along, 0.5 * v_across, 0.25 * (u_across + v_along),
            jnp.concatenate([p_ym, p_yp], axis=0),
        )

        visc_t = visc.T
        north = jnp.sqrt(visc * above(visc, 1, visc_y[1:]))
        south = jnp.sqrt(visc * below(visc, 1, visc_y[:1]))
        east = jnp.sqrt(visc_t * above(visc_t, 1, visc_x[1:]))
        west = jnp.sqrt(visc_t * below(visc_t, 1, visc_x[:1]))

        excess = (ice_mass + weak * (north + south)).T
        right = (
            ice_mass * u + wind_x + CORIOLIS * ice_mass * v
            + weak * (north * u_north + south * u_south)
        ).T - press_x
        first, steps, p, q, f = reduce_matrix(
            jnp.where(live_t, west, 0.0),
            jnp.where(live_t, excess, 1.0),
            jnp.where(live_t, east, 0.0),
        )
        gather_start("gx", x_ends[0], sweep, ends_matrix(p, q, f))
        g = reduce_right(jnp.where(live_t, right, 0.0), first, steps)
        gather_start("gx", x_ends[1], sweep, ends_right(g))

        @pl.when(me["gx"] >= 0)
        def _():
            excess = ice_mass + (weak * (east + west)).T
            first, steps, p_y, q_y, f_y = reduce_matrix(
                jnp.where(live, south, 0.0),
                jnp.where(live, excess, 1.0),
                jnp.where(live, north, 0.0),
            )
            gather_start("gy", y_ends[0], sweep, ends_matrix(p_y, q_y, f_y))
            for n, (_, p_n, q_n, inv) in enumerate(steps):
                y_steps[n, 0], y_steps[n, 1], y_steps[n, 2] = p_n, q_n, inv
            right = (
                ice_mass * v + wind_y
                + (weak * (east * v_east + west * v_west)).T
                - press_y
            )
            y_rest[0], y_rest[1], y_rest[2], y_rest[3] = first, p_y, q_y, right

        u_xm, u_xp = outer_values("gx", *x_ends, sweep)
        u_t = g + p * u_xm + q * u_xp
        u = u_t.T
        if sweep + 1 < PASSES:
            early = 2 * sweep + 1
            halo_fill(early, YM, (u[:1], u[1:2]))
            halo_fill(early, YP, (u[-1:], u[-2:-1]))
            halo_start(early, YM)
            halo_start(early, YP)
        else:
            out[0] = u
        y_strides = [
            (2**n, y_steps[n, 0], y_steps[n, 1], y_steps[n, 2])
            for n in range(y_steps.shape[0])
        ]
        right = y_rest[3] - CORIOLIS * ice_mass * u
        g = reduce_right(jnp.where(live, right, 0.0), y_rest[0], y_strides)
        gather_start("gy", y_ends[1], sweep, ends_right(g))
        v_ym, v_yp = outer_values("gy", *y_ends, sweep)
        v = g + y_rest[1] * v_ym + y_rest[2] * v_yp
        if sweep + 1 < PASSES:
            late = early + 1
            halo_fill(late, YM, (v[1:2],))
            halo_fill(late, YP, (v[-2:-1],))
            halo_start(late, YM)
            halo_start(late, YP)
            u_ym, u_ym2 = halo_wait(early, YM, 2)
            u_yp, u_yp2 = halo_wait(early, YP, 2)
            v_t = v.T
            for direction, near, next_, lane in ((XM, 0, 1, 0), (XP, cx - 1, cx - 2, cx - 1)):
                rows = [
                    u_t[near : near + 1], v_t[near : near + 1],
                    u_t[next_ : next_ + 1], v_t[next_ : next_ + 1],
                ] + [
                    jnp.broadcast_to(row[:, lane : lane + 1], (1, halo_out.shape[3]))
                    for row in (u_ym, v_ym, u_yp, v_yp)
                ]
                halo_fill(late, direction, rows)
                halo_start(late, direction)
    out[1] = v
    for sweep in range(PASSES):
        for name, ends in gathers:
            for k in range(1, sizes[name]):
                ends_copy(name, ends, sweep, k, me[name]).wait_send()


def on_device(sizes, velocity, wind_stress, thickness, ice_mask, land_mask):
    cy, cx = thickness.shape
    wide = max(cx, cy)
    nx, ny = sizes["gx"], sizes["gy"]
    slots = 2 * PASSES - 1
    dma = pltpu.SemaphoreType.DMA
    strides = (cy - 1).bit_length()
    f32 = jnp.float32
    args = (velocity, wind_stress, thickness, ice_mask, land_mask)
    return pl.pallas_call(
        functools.partial(kernel, sizes),
        out_shape=pltpu.VMEM(velocity.shape, f32),
        in_specs=[pl.BlockSpec(memory_space=pl.ANY)] * 5,
        out_specs=pl.BlockSpec(memory_space=pltpu.VMEM),
        scratch_shapes=[pltpu.VMEM(arg.shape, arg.dtype) for arg in args]
        + [
            dma((5,)),
            pltpu.VMEM((slots, 4, 8, wide), f32),
            pltpu.VMEM((slots, 4, 8, wide), f32),
            pltpu.VMEM((4, 2, wide), f32),
            pltpu.VMEM((4, 2, wide), f32),
            pltpu.VMEM((PASSES, nx, 6, cy), f32),
            pltpu.VMEM((PASSES, nx, 2, cy), f32),
            pltpu.VMEM((PASSES, ny, 6, cx), f32),
            pltpu.VMEM((PASSES, ny, 2, cx), f32),
            pltpu.VMEM((strides, 3, cy, cx), f32),
            pltpu.VMEM((4, cy, cx), f32),
            dma((slots, 4)), dma((slots, 4)), dma((4,)), dma((4,)),
        ]
        + [dma((PASSES, nx - 1))] * 4
        + [dma((PASSES, ny - 1))] * 4,
        compiler_params=pltpu.CompilerParams(collective_id=0, has_side_effects=True),
        name="ice_relaxation",
    )(*args)


def solution(mesh):
    sizes = {name: int(mesh.shape[name]) for name in ("gx", "gy")}
    cells = P("gy", "gx")
    pairs = P(None, "gy", "gx")
    return jax.shard_map(
        functools.partial(on_device, sizes),
        mesh=mesh,
        in_specs=(pairs, pairs, cells, cells, cells),
        out_specs=pairs,
        check_vma=False,
    )
```

```python
import functools

import jax
import jax.numpy as jnp
from jax import lax
from jax.experimental import pallas as pl
from jax.experimental.pallas import tpu as pltpu
from jax.sharding import PartitionSpec as P

PASSES = 2
CORIOLIS = 1.0
DELTA_MIN = 0.25
WIND_GAIN = 0.2
MESH = pl.DeviceIdType.MESH

XM, XP, YM, YP = 0, 1, 2, 3
AXIS = ("gx", "gx", "gy", "gy")
STEP = (-1, 1, -1, 1)


def below(array, stride, fill):
    rows = array.shape[0]
    if stride % 8 == 0:
        filler = jnp.broadcast_to(jnp.float32(fill), (stride, array.shape[1]))
        return jnp.concatenate([filler, array[:-stride]], axis=0)
    row = lax.broadcasted_iota(jnp.int32, array.shape, 0)
    return jnp.where(row < stride, fill, pltpu.roll(array, stride, 0))


def above(array, stride, fill):
    rows = array.shape[0]
    if stride % 8 == 0:
        filler = jnp.broadcast_to(jnp.float32(fill), (stride, array.shape[1]))
        return jnp.concatenate([array[stride:], filler], axis=0)
    row = lax.broadcasted_iota(jnp.int32, array.shape, 0)
    return jnp.where(row >= rows - stride, fill, pltpu.roll(array, rows - stride, 0))


def reduce_matrix(low, excess, high):
    inv = 1.0 / (excess + low + high)
    first = inv
    p, q, f = low * inv, high * inv, excess * inv
    steps = []
    stride = 1
    while stride < low.shape[0]:
        p_next = p * below(p, stride, 1.0)
        q_next = q * above(q, stride, 1.0)
        f_next = f + p * below(f, stride, 0.0) + q * above(f, stride, 0.0)
        inv = 1.0 / (f_next + p_next + q_next)
        steps.append((stride, p, q, inv))
        p, q, f = p_next * inv, q_next * inv, f_next * inv
        stride *= 2
    return first, steps, p, q, f


def reduce_right(right, first, steps):
    g = right * first
    for stride, p, q, inv in steps:
        g = (g + p * below(g, stride, 0.0) + q * above(g, stride, 0.0)) * inv
    return g


def ends_matrix(p, q, f):
    return jnp.concatenate([p[:1], q[:1], f[:1], p[-1:], q[-1:], f[-1:]], axis=0)


def ends_right(g):
    return jnp.concatenate([g[:1], g[-1:]], axis=0)


def link(matrix, b, c):
    p0, q0, f0, p1, q1, f1 = matrix
    inv = 1.0 / (f0 + q0 + p0 * c)
    head_b = q0 * inv
    head_c = (f0 + p0 * c) * inv
    through = p1 * b * inv
    gains = (p1 + through * p0, through)
    return q1 + p1 * (b * head_b), f1 + p1 * (c + b * head_c), gains, (inv, head_b)


def chain_matrix(matrix_of, me, count):
    mine = matrix_of(me)
    zero = jnp.zeros_like(mine[0])
    lb, lc, rb, rc = zero, zero + 1.0, zero, zero + 1.0
    links = []
    beyond = [(zero,) * 4] * 2
    for j in range(count - 1):
        ends = matrix_of(j)
        nb, nc, gains, (inv, head_b) = link(ends, lb, lc)
        keep = (lb, inv, head_b, ends[0] * inv)
        beyond[0] = [jnp.where(j == me - 1, n, o) for n, o in zip(keep, beyond[0])]
        take = j < me
        lb, lc = jnp.where(take, nb, lb), jnp.where(take, nc, lc)
        k = count - 1 - j
        p0, q0, f0, p1, q1, f1 = matrix_of(k)
        nb, nc, back, (inv, head_b) = link((q1, p1, f1, q0, p0, f0), rb, rc)
        keep = (rb, inv, head_b, q1 * inv)
        beyond[1] = [jnp.where(k == me + 1, n, o) for n, o in zip(keep, beyond[1])]
        take = k > me
        rb, rc = jnp.where(take, nb, rb), jnp.where(take, nc, rc)
        links.append((gains, back))
    b, c, gains, (inv, head_b) = link(mine, lb, lc)
    last_inv = 1.0 / (c + b * rc)
    return links, beyond, gains, mine[0] * inv, inv, head_b, lb, b, rb, last_inv


def chain_right(right_of, chain, me, count):
    links, beyond, gains, p0_inv, inv, head_b, left_b, b, rb, last_inv = chain
    mine = right_of(me)
    left = right = jnp.zeros_like(mine[0])
    kept = [(left, left), (left, left)]
    for j, (ahead, back) in enumerate(links):
        g0, g1 = right_of(j)
        kept[0] = [jnp.where(j == me - 1, n, o) for n, o in zip((left, g0), kept[0])]
        left = jnp.where(j < me, g1 + ahead[0] * left + ahead[1] * g0, left)
        k = count - 1 - j
        g0, g1 = right_of(k)
        kept[1] = [jnp.where(k == me + 1, n, o) for n, o in zip((right, g1), kept[1])]
        right = jnp.where(k > me, g0 + back[0] * right + back[1] * g1, right)
    a = mine[1] + gains[0] * left + gains[1] * mine[0]
    last = (a + b * right) * last_inv
    after = right + rb * last
    first = mine[0] * inv + p0_inv * left + head_b * after
    before = left + left_b * first
    far = [
        a_n + b_n * (g_n * inv_n + p_n * a_n + h_n * own)
        for (a_n, g_n), (b_n, inv_n, h_n, p_n), own in zip(kept, beyond, (first, last))
    ]
    return before, after, far


def lane_below(row, corner):
    lane = lax.broadcasted_iota(jnp.int32, row.shape, 1)
    return jnp.where(lane == 0, corner, pltpu.roll(row, 1, 1))


def lane_above(row, corner):
    lane = lax.broadcasted_iota(jnp.int32, row.shape, 1)
    return jnp.where(
        lane == row.shape[1] - 1, corner, pltpu.roll(row, row.shape[1] - 1, 1)
    )


def viscosity_of(strain_xx, strain_yy, shear, thickness):
    delta2 = (
        1.25 * (strain_xx * strain_xx + strain_yy * strain_yy)
        + shear * shear
        + 1.5 * strain_xx * strain_yy
    )
    return thickness / (2.0 * jnp.sqrt(delta2 + DELTA_MIN * DELTA_MIN))


def kernel(
    sizes,
    velocity_hbm, wind_hbm, thickness_hbm, ice_hbm, land_hbm,
    out,
    velocity, wind, thickness_ref, ice, land, in_sem,
    halo_out, halo_in, diag_out, diag_in,
    x_matrix, x_right, y_matrix, y_right, y_steps, y_rest,
    halo_send, halo_recv, diag_send, diag_recv,
    xm_send, xm_recv, xr_send, xr_recv, ym_send, ym_recv, yr_send, yr_recv,
    sm_send, sm_recv, sr_send, sr_recv,
):
    me = {name: lax.axis_index(name) for name in ("gx", "gy")}
    loads = [
        pltpu.make_async_copy(src, dst, in_sem.at[n])
        for n, (src, dst) in enumerate(
            (
                (velocity_hbm, velocity), (thickness_hbm, thickness_ref),
                (wind_hbm, wind), (ice_hbm, ice), (land_hbm, land),
            )
        )
    ]
    for load in loads:
        load.start()

    def has(direction):
        name = AXIS[direction]
        if STEP[direction] < 0:
            return me[name] > 0
        return me[name] < sizes[name] - 1

    corners = [(x, y) for x in (XM, XP) for y in (YM, YP)]

    def corner_id(x, y):
        return {"gx": me["gx"] + STEP[x], "gy": me["gy"] + STEP[y]}

    def has_corner(x, y):
        return jnp.logical_and(has(x), has(y))

    def side_id(side, k):
        return {
            "gx": me["gx"] + STEP[side],
            "gy": lax.rem(me["gy"] + k, sizes["gy"]),
        }

    barrier = pltpu.get_barrier_semaphore()
    total = 0
    for name in ("gx", "gy"):
        for k in range(1, sizes[name]):
            pl.semaphore_signal(
                barrier,
                device_id={name: lax.rem(me[name] + k, sizes[name])},
                device_id_type=MESH,
            )
            total += 1
    for side in (XM, XP):
        total = total + jnp.where(has(side), sizes["gy"] - 1, 0)

        @pl.when(has(side))
        def _():
            for k in range(1, sizes["gy"]):
                pl.semaphore_signal(
                    barrier, device_id=side_id(side, k), device_id_type=MESH
                )

    def halo_copy(slot, direction, landing):
        return pltpu.make_async_remote_copy(
            src_ref=halo_out.at[slot, direction],
            dst_ref=halo_in.at[slot, landing],
            send_sem=halo_send.at[slot, direction],
            recv_sem=halo_recv.at[slot, landing],
            device_id={AXIS[direction]: me[AXIS[direction]] + STEP[direction]},
            device_id_type=MESH,
        )

    def halo_fill(slot, direction, rows, start=0):
        for n, row in enumerate(rows, start):
            halo_out[slot, direction, n : n + 1, : row.shape[1]] = row

    def halo_start(slot, direction):
        @pl.when(has(direction))
        def _():
            halo_copy(slot, direction, direction ^ 1).start()

    def halo_wait(slot, direction, count):
        @pl.when(has(direction))
        def _():
            halo_copy(slot, direction, direction).wait()

        wide = cy if AXIS[direction] == "gx" else cx
        block = jnp.where(has(direction), halo_in[slot, direction, :, :wide], 0.0)
        return [block[n : n + 1] for n in range(count)]

    def diag_copy(n, landing):
        return pltpu.make_async_remote_copy(
            src_ref=diag_out.at[n],
            dst_ref=diag_in.at[landing],
            send_sem=diag_send.at[n],
            recv_sem=diag_recv.at[landing],
            device_id=corner_id(*corners[n]),
            device_id_type=MESH,
        )

    def ends_copy(name, ends, sweep, k, source):
        buf, send, recv = ends
        return pltpu.make_async_remote_copy(
            src_ref=buf.at[sweep, source, 0],
            dst_ref=buf.at[sweep, source, 0],
            send_sem=send.at[sweep, k - 1],
            recv_sem=recv.at[sweep, k - 1],
            device_id={name: lax.rem(me[name] + k, sizes[name])},
            device_id_type=MESH,
        )

    def side_copy(ends, sides, sweep, side, k, source, landing):
        buf, (send, recv) = ends[0], sides
        return pltpu.make_async_remote_copy(
            src_ref=buf.at[sweep, source, 0],
            dst_ref=buf.at[sweep, source, 1 + landing],
            send_sem=send.at[sweep, side, k],
            recv_sem=recv.at[sweep, landing, k],
            device_id=side_id(side, k),
            device_id_type=MESH,
        )

    def gather_start(name, ends, sweep, block, sides=None):
        ends[0][sweep, me[name], 0] = block
        for k in range(1, sizes[name]):
            ends_copy(name, ends, sweep, k, me[name]).start()
        if sides is not None:
            for side in (XM, XP):

                @pl.when(has(side))
                def _():
                    for k in range(sizes["gy"]):
                        side_copy(
                            ends, sides, sweep, side, k, me["gy"], side ^ 1
                        ).start()

    def gather_wait(name, ends, sweep, sides=None):
        count = sizes[name]
        for k in range(1, count):
            source = lax.rem(me[name] + count - k, count)
            ends_copy(name, ends, sweep, k, source).wait_recv()
        if sides is not None:
            for side in (XM, XP):

                @pl.when(has(side))
                def _():
                    for k in range(count):
                        source = lax.rem(me[name] + count - k, count)
                        side_copy(
                            ends, sides, sweep, side, k, source, side
                        ).wait_recv()

        def block_of(j):
            blocks = [ends[0][sweep, j, n] for n in range(1 if sides is None else 3)]
            return [
                jnp.concatenate([block[n : n + 1] for block in blocks], axis=0)
                for n in range(blocks[0].shape[0])
            ]

        return block_of

    def outer_values(name, matrix, right, sweep, sides=(None, None)):
        chain = chain_matrix(
            gather_wait(name, matrix, sweep, sides[0]), me[name], sizes[name]
        )
        return chain_right(
            gather_wait(name, right, sweep, sides[1]), chain, me[name], sizes[name]
        )

    gathers = (
        ("gx", (x_matrix, xm_send, xm_recv)),
        ("gx", (x_right, xr_send, xr_recv)),
        ("gy", (y_matrix, ym_send, ym_recv)),
        ("gy", (y_right, yr_send, yr_recv)),
    )
    x_ends = (gathers[0][1], gathers[1][1])
    y_ends = (gathers[2][1], gathers[3][1])

    side_sems = ((sm_send, sm_recv), (sr_send, sr_recv))
    cy, cx = thickness_ref.shape
    cell_count = float(cy * cx)
    weak = 1.0 / (16.0 * cell_count)
    press = cell_count ** (-0.25)
    drive = WIND_GAIN * cell_count ** (-0.75)

    loads[0].wait()
    loads[1].wait()
    u, v = velocity[0], velocity[1]
    thickness = thickness_ref[...]
    u_t, v_t, thickness_t = u.T, v.T, thickness.T
    halo_fill(0, YM, (u[:1], v[:1], u[1:2], v[1:2], thickness[:1]))
    halo_fill(0, YP, (u[-1:], v[-1:], u[-2:-1], v[-2:-1], thickness[-1:]))
    for n, (x, y) in enumerate(corners):
        row = slice(0, 1) if y == YM else slice(cy - 1, cy)
        lane = slice(0, 1) if x == XM else slice(cx - 1, cx)
        for m, field in enumerate((u, v)):
            diag_out[n, m : m + 1, :] = jnp.broadcast_to(
                field[row, lane], (1, diag_out.shape[2])
            )
    halo_fill(0, XM, (u_t[:1], v_t[:1], u_t[1:2], v_t[1:2], thickness_t[:1]))
    halo_fill(0, XP, (u_t[-1:], v_t[-1:], u_t[-2:-1], v_t[-2:-1], thickness_t[-1:]))
    pl.semaphore_wait(barrier, total)
    for n in range(4):

        @pl.when(has_corner(*corners[n]))
        def _():
            diag_copy(n, 3 - n).start()

    for direction in (YM, YP, XM, XP):
        halo_start(0, direction)

    for load in loads[2:]:
        load.wait()
    active = (ice[...] * (1 - land[...])).astype(jnp.float32)
    live = active > 0.5
    live_t = active.T > 0.5
    ice_mass = weak * thickness
    wind_x = drive * wind[0]
    wind_y = drive * wind[1]

    for sweep in range(PASSES):
        more = sweep + 1 < PASSES
        early, late = 2 * sweep + 1, 2 * sweep + 2
        sides = side_sems if more else (None, None)
        if sweep == 0:
            u_xm, v_xm, u_xm2, v_xm2, p_xm = halo_wait(0, XM, 5)
            u_xp, v_xp, u_xp2, v_xp2, p_xp = halo_wait(0, XP, 5)
            u_ym, v_ym, u_ym2, v_ym2, p_ym = halo_wait(0, YM, 5)
            u_yp, v_yp, u_yp2, v_yp2, p_yp = halo_wait(0, YP, 5)
            corner = []
            for n in range(4):

                @pl.when(has_corner(*corners[n]))
                def _():
                    diag_copy(n, n).wait()

                block = jnp.where(has_corner(*corners[n]), diag_in[n], 0.0)
                corner.append([block[:1], block[1:2]])
            mm, mp, pm, pp = corner
            press_x = 0.5 * press * (
                above(thickness_t, 1, p_xp) - below(thickness_t, 1, p_xm)
            )
            press_y = 0.5 * press * (
                above(thickness, 1, p_yp) - below(thickness, 1, p_ym)
            )

        v_east, v_west = above(v_t, 1, v_xp), below(v_t, 1, v_xm)
        u_north, u_south = above(u, 1, u_yp), below(u, 1, u_ym)
        strain_xx = (0.5 * (above(u_t, 1, u_xp) - below(u_t, 1, u_xm))).T
        strain_yy = 0.5 * (above(v, 1, v_yp) - below(v, 1, v_ym))
        shear = 0.25 * ((u_north - u_south) + (v_east - v_west).T)
        visc = viscosity_of(strain_xx, strain_yy, shear, thickness)

        def rim(near, minus1, minus2, plus1, plus2, m_lo, m_hi, p_lo, p_hi):
            across = jnp.concatenate([near[:1] - minus2, plus2 - near[-1:]], axis=0)
            n = minus1.shape[1]
            along = jnp.concatenate(
                [
                    lane_above(minus1, m_hi[:, :n]) - lane_below(minus1, m_lo[:, :n]),
                    lane_above(plus1, p_hi[:, :n]) - lane_below(plus1, p_lo[:, :n]),
                ],
                axis=0,
            )
            return across, along

        u_across, u_along = rim(
            u_t, u_xm, u_xm2, u_xp, u_xp2, mm[0], mp[0], pm[0], pp[0]
        )
        v_across, v_along = rim(
            v_t, v_xm, v_xm2, v_xp, v_xp2, mm[1], mp[1], pm[1], pp[1]
        )
        visc_x = viscosity_of(
            0.5 * u_across, 0.5 * v_along, 0.25 * (u_along + v_across),
            jnp.concatenate([p_xm, p_xp], axis=0),
        )
        u_across, u_along = rim(
            u, u_ym, u_ym2, u_yp, u_yp2, mm[0], pm[0], mp[0], pp[0]
        )
        v_across, v_along = rim(
            v, v_ym, v_ym2, v_yp, v_yp2, mm[1], pm[1], mp[1], pp[1]
        )
        visc_y = viscosity_of(
            0.5 * u_along, 0.5 * v_across, 0.25 * (u_across + v_along),
            jnp.concatenate([p_ym, p_yp], axis=0),
        )

        visc_t = visc.T
        north = jnp.sqrt(visc * above(visc, 1, visc_y[1:]))
        south = jnp.sqrt(visc * below(visc, 1, visc_y[:1]))
        east = jnp.sqrt(visc_t * above(visc_t, 1, visc_x[1:]))
        west = jnp.sqrt(visc_t * below(visc_t, 1, visc_x[:1]))

        excess = (ice_mass + weak * (north + south)).T
        right = (
            ice_mass * u + wind_x + CORIOLIS * ice_mass * v
            + weak * (north * u_north + south * u_south)
        ).T - press_x
        first, steps, p, q, f = reduce_matrix(
            jnp.where(live_t, west, 0.0),
            jnp.where(live_t, excess, 1.0),
            jnp.where(live_t, east, 0.0),
        )
        gather_start("gx", x_ends[0], sweep, ends_matrix(p, q, f))
        g = reduce_right(jnp.where(live_t, right, 0.0), first, steps)
        gather_start("gx", x_ends[1], sweep, ends_right(g))

        @pl.when(me["gx"] >= 0)
        def _():
            excess = ice_mass + (weak * (east + west)).T
            first, steps, p_y, q_y, f_y = reduce_matrix(
                jnp.where(live, south, 0.0),
                jnp.where(live, excess, 1.0),
                jnp.where(live, north, 0.0),
            )
            gather_start("gy", y_ends[0], sweep, ends_matrix(p_y, q_y, f_y), sides[0])
            for n, (_, p_n, q_n, inv) in enumerate(steps):
                y_steps[n, 0], y_steps[n, 1], y_steps[n, 2] = p_n, q_n, inv
            right = (
                ice_mass * v + wind_y
                + (weak * (east * v_east + west * v_west)).T
                - press_y
            )
            y_rest[0], y_rest[1], y_rest[2], y_rest[3] = first, p_y, q_y, right
            if more:
                p_t, q_t = p_y.T, q_y.T
                halo_fill(late, XM, (p_t[:1], q_t[:1], p_t[1:2], q_t[1:2]))
                halo_fill(late, XP, (p_t[-1:], q_t[-1:], p_t[-2:-1], q_t[-2:-1]))
                halo_fill(late, YM, (p_y[1:2], q_y[1:2]))
                halo_fill(late, YP, (p_y[-2:-1], q_y[-2:-1]))

        u_xm, u_xp, _ = outer_values("gx", *x_ends, sweep)
        u_t = g + p * u_xm + q * u_xp
        u = u_t.T
        y_strides = [
            (2**n, y_steps[n, 0], y_steps[n, 1], y_steps[n, 2])
            for n in range(y_steps.shape[0])
        ]
        right = y_rest[3] - CORIOLIS * ice_mass * u
        g = reduce_right(jnp.where(live, right, 0.0), y_rest[0], y_strides)
        gather_start("gy", y_ends[1], sweep, ends_right(g), sides[1])
        if more:
            wide = halo_out.shape[3]
            spread = lambda row, n: jnp.broadcast_to(row[:, n : n + 1], (1, wide))
            halo_fill(late, YM, (g[1:2],), 2)
            halo_fill(late, YP, (g[-2:-1],), 2)
            halo_fill(early, YM, (u[:1], u[1:2], spread(u_xm, 0), spread(u_xp, 0)))
            halo_fill(
                early, YP,
                (u[-1:], u[-2:-1], spread(u_xm, cy - 1), spread(u_xp, cy - 1)),
            )
            halo_fill(early, XM, (u_t[1:2],))
            halo_fill(early, XP, (u_t[-2:-1],))
            for direction in (YM, YP):
                halo_start(early, direction)
                halo_start(late, direction)
            g_t = g.T
            halo_fill(late, XM, (g_t[:1], g_t[1:2]), 4)
            halo_fill(late, XP, (g_t[-1:], g_t[-2:-1]), 4)
            for direction in (XM, XP):
                halo_start(early, direction)
                halo_start(late, direction)
        else:
            out[0] = u
        before, after, far = outer_values("gy", *y_ends, sweep, sides)
        v_ym, v_yp = before[:1], after[:1]
        v = g + y_rest[1] * v_ym + y_rest[2] * v_yp
        if more:
            v_t = v.T
            u_ym, u_ym2, *low = halo_wait(early, YM, 4)
            u_yp, u_yp2, *high = halo_wait(early, YP, 4)
            (u_xm2,) = halo_wait(early, XM, 1)
            (u_xp2,) = halo_wait(early, XP, 1)
            p_2, q_2, g_2 = halo_wait(late, YM, 3)
            v_ym2 = jnp.where(has(YM), g_2 + p_2 * far[0][:1] + q_2 * v[:1], 0.0)
            p_2, q_2, g_2 = halo_wait(late, YP, 3)
            v_yp2 = jnp.where(has(YP), g_2 + p_2 * v[-1:] + q_2 * far[1][:1], 0.0)

            def beside(direction, row, lanes):
                p_1, q_1, p_2, q_2, g_1, g_2 = halo_wait(late, direction, 6)
                lo, hi = (
                    [jnp.where(has(direction), end[row : row + 1, n : n + 1], 0.0) for n in lanes]
                    for end in (before, after)
                )
                near = g_1 + p_1 * lo[0] + q_1 * hi[0]
                next_ = g_2 + p_2 * lo[1] + q_2 * hi[1]
                return near, next_, lo[0], hi[0]

            v_xm, v_xm2, mm_v, mp_v = beside(XM, 1, (cx - 1, cx - 2))
            v_xp, v_xp2, pm_v, pp_v = beside(XP, 2, (0, 1))
            mm, mp = (low[0], mm_v), (high[0], mp_v)
            pm, pp = (low[1], pm_v), (high[1], pp_v)
    out[1] = v
    for sweep in range(PASSES):
        for name, ends in gathers:
            for k in range(1, sizes[name]):
                ends_copy(name, ends, sweep, k, me[name]).wait_send()
    for sweep in range(PASSES - 1):
        for ends, sides in zip(y_ends, side_sems):
            for side in (XM, XP):

                @pl.when(has(side))
                def _():
                    for k in range(sizes["gy"]):
                        side_copy(
                            ends, sides, sweep, side, k, me["gy"], side ^ 1
                        ).wait_send()


def on_device(sizes, velocity, wind_stress, thickness, ice_mask, land_mask):
    cy, cx = thickness.shape
    wide = max(cx, cy)
    nx, ny = sizes["gx"], sizes["gy"]
    slots = 2 * PASSES - 1
    dma = pltpu.SemaphoreType.DMA
    strides = (cy - 1).bit_length()
    f32 = jnp.float32
    args = (velocity, wind_stress, thickness, ice_mask, land_mask)
    return pl.pallas_call(
        functools.partial(kernel, sizes),
        out_shape=pltpu.VMEM(velocity.shape, f32),
        in_specs=[pl.BlockSpec(memory_space=pl.ANY)] * 5,
        out_specs=pl.BlockSpec(memory_space=pltpu.VMEM),
        scratch_shapes=[pltpu.VMEM(arg.shape, arg.dtype) for arg in args]
        + [
            dma((5,)),
            pltpu.VMEM((slots, 4, 8, wide), f32),
            pltpu.VMEM((slots, 4, 8, wide), f32),
            pltpu.VMEM((4, 2, wide), f32),
            pltpu.VMEM((4, 2, wide), f32),
            pltpu.VMEM((PASSES, nx, 1, 6, cy), f32),
            pltpu.VMEM((PASSES, nx, 1, 2, cy), f32),
            pltpu.VMEM((PASSES, ny, 3, 6, cx), f32),
            pltpu.VMEM((PASSES, ny, 3, 2, cx), f32),
            pltpu.VMEM((strides, 3, cy, cx), f32),
            pltpu.VMEM((4, cy, cx), f32),
            dma((slots, 4)), dma((slots, 4)), dma((4,)), dma((4,)),
        ]
        + [dma((PASSES, nx - 1))] * 4
        + [dma((PASSES, ny - 1))] * 4
        + [dma((PASSES, 2, ny))] * 4,
        compiler_params=pltpu.CompilerParams(collective_id=0, has_side_effects=True),
        name="ice_relaxation",
    )(*args)


def solution(mesh):
    sizes = {name: int(mesh.shape[name]) for name in ("gx", "gy")}
    cells = P("gy", "gx")
    pairs = P(None, "gy", "gx")
    return jax.shard_map(
        functools.partial(on_device, sizes),
        mesh=mesh,
        in_specs=(pairs, pairs, cells, cells, cells),
        out_specs=pairs,
        check_vma=False,
    )
```

```python
import functools

import jax
import jax.numpy as jnp
from jax import lax
from jax.experimental import pallas as pl
from jax.experimental.pallas import tpu as pltpu
from jax.sharding import PartitionSpec as P

PASSES = 2
CORIOLIS = 1.0
DELTA_MIN = 0.25
WIND_GAIN = 0.2
MESH = pl.DeviceIdType.MESH

XM, XP, YM, YP = 0, 1, 2, 3
AXIS = ("gx", "gx", "gy", "gy")
STEP = (-1, 1, -1, 1)


def below(array, stride, fill):
    rows = array.shape[0]
    if stride % 8 == 0:
        filler = jnp.broadcast_to(jnp.float32(fill), (stride, array.shape[1]))
        return jnp.concatenate([filler, array[:-stride]], axis=0)
    row = lax.broadcasted_iota(jnp.int32, array.shape, 0)
    return jnp.where(row < stride, fill, pltpu.roll(array, stride, 0))


def above(array, stride, fill):
    rows = array.shape[0]
    if stride % 8 == 0:
        filler = jnp.broadcast_to(jnp.float32(fill), (stride, array.shape[1]))
        return jnp.concatenate([array[stride:], filler], axis=0)
    row = lax.broadcasted_iota(jnp.int32, array.shape, 0)
    return jnp.where(row >= rows - stride, fill, pltpu.roll(array, rows - stride, 0))


def reduce_matrix(low, excess, high):
    inv = 1.0 / (excess + low + high)
    first = inv
    p, q, f = low * inv, high * inv, excess * inv
    steps = []
    stride = 1
    while stride < low.shape[0]:
        p_next = p * below(p, stride, 1.0)
        q_next = q * above(q, stride, 1.0)
        f_next = f + p * below(f, stride, 0.0) + q * above(f, stride, 0.0)
        inv = 1.0 / (f_next + p_next + q_next)
        steps.append((stride, p, q, inv))
        p, q, f = p_next * inv, q_next * inv, f_next * inv
        stride *= 2
    return first, steps, p, q, f


def reduce_right(right, first, steps):
    g = right * first
    for stride, p, q, inv in steps:
        g = (g + p * below(g, stride, 0.0) + q * above(g, stride, 0.0)) * inv
    return g


def ends_matrix(p, q, f):
    return jnp.concatenate([p[:1], q[:1], f[:1], p[-1:], q[-1:], f[-1:]], axis=0)


def ends_right(g):
    return jnp.concatenate([g[:1], g[-1:]], axis=0)


def link(matrix, b, c):
    p0, q0, f0, p1, q1, f1 = matrix
    inv = 1.0 / (f0 + q0 + p0 * c)
    head_b = q0 * inv
    head_c = (f0 + p0 * c) * inv
    through = p1 * b * inv
    gains = (p1 + through * p0, through)
    return q1 + p1 * (b * head_b), f1 + p1 * (c + b * head_c), gains, (inv, head_b)


def chain_matrix(matrix_of, me, count):
    mine = matrix_of(me)
    zero = jnp.zeros_like(mine[0])
    lb, lc, rb, rc = zero, zero + 1.0, zero, zero + 1.0
    links = []
    beyond = [(zero,) * 4] * 2
    for j in range(count - 1):
        ends = matrix_of(j)
        nb, nc, gains, (inv, head_b) = link(ends, lb, lc)
        keep = (lb, inv, head_b, ends[0] * inv)
        beyond[0] = [jnp.where(j == me - 1, n, o) for n, o in zip(keep, beyond[0])]
        take = j < me
        lb, lc = jnp.where(take, nb, lb), jnp.where(take, nc, lc)
        k = count - 1 - j
        p0, q0, f0, p1, q1, f1 = matrix_of(k)
        nb, nc, back, (inv, head_b) = link((q1, p1, f1, q0, p0, f0), rb, rc)
        keep = (rb, inv, head_b, q1 * inv)
        beyond[1] = [jnp.where(k == me + 1, n, o) for n, o in zip(keep, beyond[1])]
        take = k > me
        rb, rc = jnp.where(take, nb, rb), jnp.where(take, nc, rc)
        links.append((gains, back))
    b, c, gains, (inv, head_b) = link(mine, lb, lc)
    last_inv = 1.0 / (c + b * rc)
    return links, beyond, gains, mine[0] * inv, inv, head_b, lb, b, rb, last_inv


def chain_right(right_of, chain, me, count):
    links, beyond, gains, p0_inv, inv, head_b, left_b, b, rb, last_inv = chain
    mine = right_of(me)
    left = right = jnp.zeros_like(mine[0])
    kept = [(left, left), (left, left)]
    for j, (ahead, back) in enumerate(links):
        g0, g1 = right_of(j)
        kept[0] = [jnp.where(j == me - 1, n, o) for n, o in zip((left, g0), kept[0])]
        left = jnp.where(j < me, g1 + ahead[0] * left + ahead[1] * g0, left)
        k = count - 1 - j
        g0, g1 = right_of(k)
        kept[1] = [jnp.where(k == me + 1, n, o) for n, o in zip((right, g1), kept[1])]
        right = jnp.where(k > me, g0 + back[0] * right + back[1] * g1, right)
    a = mine[1] + gains[0] * left + gains[1] * mine[0]
    last = (a + b * right) * last_inv
    after = right + rb * last
    first = mine[0] * inv + p0_inv * left + head_b * after
    before = left + left_b * first
    far = [
        a_n + b_n * (g_n * inv_n + p_n * a_n + h_n * own)
        for (a_n, g_n), (b_n, inv_n, h_n, p_n), own in zip(kept, beyond, (first, last))
    ]
    return before, after, far


def lane_below(row, corner):
    lane = lax.broadcasted_iota(jnp.int32, row.shape, 1)
    return jnp.where(lane == 0, corner, pltpu.roll(row, 1, 1))


def lane_above(row, corner):
    lane = lax.broadcasted_iota(jnp.int32, row.shape, 1)
    return jnp.where(
        lane == row.shape[1] - 1, corner, pltpu.roll(row, row.shape[1] - 1, 1)
    )


def viscosity_of(strain_xx, strain_yy, shear, thickness):
    delta2 = (
        1.25 * (strain_xx * strain_xx + strain_yy * strain_yy)
        + shear * shear
        + 1.5 * strain_xx * strain_yy
    )
    return thickness / (2.0 * jnp.sqrt(delta2 + DELTA_MIN * DELTA_MIN))


def kernel(
    sizes,
    velocity_hbm, wind_hbm, thickness_hbm, ice_hbm, land_hbm,
    out,
    velocity, wind, thickness_ref, ice, land, in_sem,
    halo_out, halo_in, diag_out, diag_in,
    x_matrix, x_right, y_matrix, y_right, y_steps, y_rest,
    halo_send, halo_recv, diag_send, diag_recv,
    xm_send, xm_recv, xr_send, xr_recv, ym_send, ym_recv, yr_send, yr_recv,
    sm_send, sm_recv, sr_send, sr_recv,
):
    me = {name: lax.axis_index(name) for name in ("gx", "gy")}
    loads = [
        pltpu.make_async_copy(src, dst, in_sem.at[n])
        for n, (src, dst) in enumerate(
            (
                (velocity_hbm, velocity), (thickness_hbm, thickness_ref),
                (wind_hbm, wind), (ice_hbm, ice), (land_hbm, land),
            )
        )
    ]
    for load in loads:
        load.start()

    def has(direction):
        name = AXIS[direction]
        if STEP[direction] < 0:
            return me[name] > 0
        return me[name] < sizes[name] - 1

    corners = [(x, y) for x in (XM, XP) for y in (YM, YP)]

    def corner_id(x, y):
        return {"gx": me["gx"] + STEP[x], "gy": me["gy"] + STEP[y]}

    def has_corner(x, y):
        return jnp.logical_and(has(x), has(y))

    def side_id(side, k):
        return {
            "gx": me["gx"] + STEP[side],
            "gy": lax.rem(me["gy"] + k, sizes["gy"]),
        }

    barrier = pltpu.get_barrier_semaphore()
    total = 0
    for name in ("gx", "gy"):
        for k in range(1, sizes[name]):
            pl.semaphore_signal(
                barrier,
                device_id={name: lax.rem(me[name] + k, sizes[name])},
                device_id_type=MESH,
            )
            total += 1
    for side in (XM, XP):
        total = total + jnp.where(has(side), sizes["gy"] - 1, 0)

        @pl.when(has(side))
        def _():
            for k in range(1, sizes["gy"]):
                pl.semaphore_signal(
                    barrier, device_id=side_id(side, k), device_id_type=MESH
                )

    def halo_copy(slot, direction, landing):
        return pltpu.make_async_remote_copy(
            src_ref=halo_out.at[slot, direction],
            dst_ref=halo_in.at[slot, landing],
            send_sem=halo_send.at[slot, direction],
            recv_sem=halo_recv.at[slot, landing],
            device_id={AXIS[direction]: me[AXIS[direction]] + STEP[direction]},
            device_id_type=MESH,
        )

    def halo_fill(slot, direction, rows, start=0):
        for n, row in enumerate(rows, start):
            halo_out[slot, direction, n : n + 1, : row.shape[1]] = row

    def halo_start(slot, direction):
        @pl.when(has(direction))
        def _():
            halo_copy(slot, direction, direction ^ 1).start()

    def halo_wait(slot, direction, count):
        @pl.when(has(direction))
        def _():
            halo_copy(slot, direction, direction).wait()

        wide = cy if AXIS[direction] == "gx" else cx
        block = jnp.where(has(direction), halo_in[slot, direction, :, :wide], 0.0)
        return [block[n : n + 1] for n in range(count)]

    def diag_copy(n, landing):
        return pltpu.make_async_remote_copy(
            src_ref=diag_out.at[n],
            dst_ref=diag_in.at[landing],
            send_sem=diag_send.at[n],
            recv_sem=diag_recv.at[landing],
            device_id=corner_id(*corners[n]),
            device_id_type=MESH,
        )

    def ends_copy(name, ends, sweep, k, source):
        buf, send, recv = ends
        return pltpu.make_async_remote_copy(
            src_ref=buf.at[sweep, source, 0],
            dst_ref=buf.at[sweep, source, 0],
            send_sem=send.at[sweep, k - 1],
            recv_sem=recv.at[sweep, k - 1],
            device_id={name: lax.rem(me[name] + k, sizes[name])},
            device_id_type=MESH,
        )

    def side_copy(ends, sides, sweep, side, k, source, landing):
        buf, (send, recv) = ends[0], sides
        return pltpu.make_async_remote_copy(
            src_ref=buf.at[sweep, source, 0],
            dst_ref=buf.at[sweep, source, 1 + landing],
            send_sem=send.at[sweep, side, k],
            recv_sem=recv.at[sweep, landing, k],
            device_id=side_id(side, k),
            device_id_type=MESH,
        )

    def gather_start(name, ends, sweep, block, sides=None):
        ends[0][sweep, me[name], 0] = block
        half = sizes[name] // 2
        for k in sorted(range(1, sizes[name]), key=lambda k: abs(k - half)):
            ends_copy(name, ends, sweep, k, me[name]).start()
        if sides is not None:
            for side in (XM, XP):

                @pl.when(has(side))
                def _():
                    for k in range(sizes["gy"]):
                        side_copy(
                            ends, sides, sweep, side, k, me["gy"], side ^ 1
                        ).start()

    def gather_wait(name, ends, sweep, sides=None):
        count = sizes[name]
        for k in range(1, count):
            source = lax.rem(me[name] + count - k, count)
            ends_copy(name, ends, sweep, k, source).wait_recv()
        if sides is not None:
            for side in (XM, XP):

                @pl.when(has(side))
                def _():
                    for k in range(count):
                        source = lax.rem(me[name] + count - k, count)
                        side_copy(
                            ends, sides, sweep, side, k, source, side
                        ).wait_recv()

        def block_of(j):
            blocks = [ends[0][sweep, j, n] for n in range(1 if sides is None else 3)]
            return [
                jnp.concatenate([block[n : n + 1] for block in blocks], axis=0)
                for n in range(blocks[0].shape[0])
            ]

        return block_of

    def outer_values(name, matrix, right, sweep, sides=(None, None)):
        chain = chain_matrix(
            gather_wait(name, matrix, sweep, sides[0]), me[name], sizes[name]
        )
        return chain_right(
            gather_wait(name, right, sweep, sides[1]), chain, me[name], sizes[name]
        )

    gathers = (
        ("gx", (x_matrix, xm_send, xm_recv)),
        ("gx", (x_right, xr_send, xr_recv)),
        ("gy", (y_matrix, ym_send, ym_recv)),
        ("gy", (y_right, yr_send, yr_recv)),
    )
    x_ends = (gathers[0][1], gathers[1][1])
    y_ends = (gathers[2][1], gathers[3][1])

    side_sems = ((sm_send, sm_recv), (sr_send, sr_recv))
    cy, cx = thickness_ref.shape
    cell_count = float(cy * cx)
    weak = 1.0 / (16.0 * cell_count)
    press = cell_count ** (-0.25)
    drive = WIND_GAIN * cell_count ** (-0.75)

    loads[0].wait()
    loads[1].wait()
    u, v = velocity[0], velocity[1]
    thickness = thickness_ref[...]
    u_t, v_t, thickness_t = u.T, v.T, thickness.T
    halo_fill(0, YM, (u[:1], v[:1], u[1:2], v[1:2], thickness[:1]))
    halo_fill(0, YP, (u[-1:], v[-1:], u[-2:-1], v[-2:-1], thickness[-1:]))
    for n, (x, y) in enumerate(corners):
        row = slice(0, 1) if y == YM else slice(cy - 1, cy)
        lane = slice(0, 1) if x == XM else slice(cx - 1, cx)
        for m, field in enumerate((u, v)):
            diag_out[n, m : m + 1, :] = jnp.broadcast_to(
                field[row, lane], (1, diag_out.shape[2])
            )
    halo_fill(0, XM, (u_t[:1], v_t[:1], u_t[1:2], v_t[1:2], thickness_t[:1]))
    halo_fill(0, XP, (u_t[-1:], v_t[-1:], u_t[-2:-1], v_t[-2:-1], thickness_t[-1:]))
    pl.semaphore_wait(barrier, total)
    for n in range(4):

        @pl.when(has_corner(*corners[n]))
        def _():
            diag_copy(n, 3 - n).start()

    for direction in (YM, YP, XM, XP):
        halo_start(0, direction)

    for load in loads[2:]:
        load.wait()
    active = (ice[...] * (1 - land[...])).astype(jnp.float32)
    live = active > 0.5
    live_t = active.T > 0.5
    ice_mass = weak * thickness
    wind_x = drive * wind[0]
    wind_y = drive * wind[1]

    for sweep in range(PASSES):
        more = sweep + 1 < PASSES
        early, late = 2 * sweep + 1, 2 * sweep + 2
        sides = side_sems if more else (None, None)
        if sweep == 0:
            u_xm, v_xm, u_xm2, v_xm2, p_xm = halo_wait(0, XM, 5)
            u_xp, v_xp, u_xp2, v_xp2, p_xp = halo_wait(0, XP, 5)
            u_ym, v_ym, u_ym2, v_ym2, p_ym = halo_wait(0, YM, 5)
            u_yp, v_yp, u_yp2, v_yp2, p_yp = halo_wait(0, YP, 5)
            corner = []
            for n in range(4):

                @pl.when(has_corner(*corners[n]))
                def _():
                    diag_copy(n, n).wait()

                block = jnp.where(has_corner(*corners[n]), diag_in[n], 0.0)
                corner.append([block[:1], block[1:2]])
            mm, mp, pm, pp = corner
            press_x = 0.5 * press * (
                above(thickness_t, 1, p_xp) - below(thickness_t, 1, p_xm)
            )
            press_y = 0.5 * press * (
                above(thickness, 1, p_yp) - below(thickness, 1, p_ym)
            )

        v_east, v_west = above(v_t, 1, v_xp), below(v_t, 1, v_xm)
        u_north, u_south = above(u, 1, u_yp), below(u, 1, u_ym)
        strain_xx = (0.5 * (above(u_t, 1, u_xp) - below(u_t, 1, u_xm))).T
        strain_yy = 0.5 * (above(v, 1, v_yp) - below(v, 1, v_ym))
        shear = 0.25 * ((u_north - u_south) + (v_east - v_west).T)
        visc = viscosity_of(strain_xx, strain_yy, shear, thickness)

        def rim(near, minus1, minus2, plus1, plus2, m_lo, m_hi, p_lo, p_hi):
            across = jnp.concatenate([near[:1] - minus2, plus2 - near[-1:]], axis=0)
            n = minus1.shape[1]
            along = jnp.concatenate(
                [
                    lane_above(minus1, m_hi[:, :n]) - lane_below(minus1, m_lo[:, :n]),
                    lane_above(plus1, p_hi[:, :n]) - lane_below(plus1, p_lo[:, :n]),
                ],
                axis=0,
            )
            return across, along

        u_across, u_along = rim(
            u_t, u_xm, u_xm2, u_xp, u_xp2, mm[0], mp[0], pm[0], pp[0]
        )
        v_across, v_along = rim(
            v_t, v_xm, v_xm2, v_xp, v_xp2, mm[1], mp[1], pm[1], pp[1]
        )
        visc_x = viscosity_of(
            0.5 * u_across, 0.5 * v_along, 0.25 * (u_along + v_across),
            jnp.concatenate([p_xm, p_xp], axis=0),
        )
        u_across, u_along = rim(
            u, u_ym, u_ym2, u_yp, u_yp2, mm[0], pm[0], mp[0], pp[0]
        )
        v_across, v_along = rim(
            v, v_ym, v_ym2, v_yp, v_yp2, mm[1], pm[1], mp[1], pp[1]
        )
        visc_y = viscosity_of(
            0.5 * u_along, 0.5 * v_across, 0.25 * (u_across + v_along),
            jnp.concatenate([p_ym, p_yp], axis=0),
        )

        visc_t = visc.T
        north = jnp.sqrt(visc * above(visc, 1, visc_y[1:]))
        south = jnp.sqrt(visc * below(visc, 1, visc_y[:1]))
        east = jnp.sqrt(visc_t * above(visc_t, 1, visc_x[1:]))
        west = jnp.sqrt(visc_t * below(visc_t, 1, visc_x[:1]))

        excess = (ice_mass + weak * (north + south)).T
        right = (
            ice_mass * u + wind_x + CORIOLIS * ice_mass * v
            + weak * (north * u_north + south * u_south)
        ).T - press_x
        first, steps, p, q, f = reduce_matrix(
            jnp.where(live_t, west, 0.0),
            jnp.where(live_t, excess, 1.0),
            jnp.where(live_t, east, 0.0),
        )
        gather_start("gx", x_ends[0], sweep, ends_matrix(p, q, f))
        g = reduce_right(jnp.where(live_t, right, 0.0), first, steps)
        gather_start("gx", x_ends[1], sweep, ends_right(g))

        @pl.when(me["gx"] >= 0)
        def _():
            excess = ice_mass + (weak * (east + west)).T
            first, steps, p_y, q_y, f_y = reduce_matrix(
                jnp.where(live, south, 0.0),
                jnp.where(live, excess, 1.0),
                jnp.where(live, north, 0.0),
            )
            gather_start("gy", y_ends[0], sweep, ends_matrix(p_y, q_y, f_y), sides[0])
            for n, (_, p_n, q_n, inv) in enumerate(steps):
                y_steps[n, 0], y_steps[n, 1], y_steps[n, 2] = p_n, q_n, inv
            right = (
                ice_mass * v + wind_y
                + (weak * (east * v_east + west * v_west)).T
                - press_y
            )
            y_rest[0], y_rest[1], y_rest[2], y_rest[3] = first, p_y, q_y, right
            if more:
                p_t, q_t = p_y.T, q_y.T
                halo_fill(late, XM, (p_t[:1], q_t[:1], p_t[1:2], q_t[1:2]))
                halo_fill(late, XP, (p_t[-1:], q_t[-1:], p_t[-2:-1], q_t[-2:-1]))
                halo_fill(late, YM, (p_y[1:2], q_y[1:2]))
                halo_fill(late, YP, (p_y[-2:-1], q_y[-2:-1]))

        u_xm, u_xp, _ = outer_values("gx", *x_ends, sweep)
        u_t = g + p * u_xm + q * u_xp
        u = u_t.T
        y_strides = [
            (2**n, y_steps[n, 0], y_steps[n, 1], y_steps[n, 2])
            for n in range(y_steps.shape[0])
        ]
        right = y_rest[3] - CORIOLIS * ice_mass * u
        g = reduce_right(jnp.where(live, right, 0.0), y_rest[0], y_strides)
        gather_start("gy", y_ends[1], sweep, ends_right(g), sides[1])
        if more:
            wide = halo_out.shape[3]
            spread = lambda row, n: jnp.broadcast_to(row[:, n : n + 1], (1, wide))
            halo_fill(late, YM, (g[1:2],), 2)
            halo_fill(late, YP, (g[-2:-1],), 2)
            halo_fill(early, YM, (u[:1], u[1:2], spread(u_xm, 0), spread(u_xp, 0)))
            halo_fill(
                early, YP,
                (u[-1:], u[-2:-1], spread(u_xm, cy - 1), spread(u_xp, cy - 1)),
            )
            halo_fill(early, XM, (u_t[1:2],))
            halo_fill(early, XP, (u_t[-2:-1],))
            for direction in (YM, YP):
                halo_start(early, direction)
                halo_start(late, direction)
            g_t = g.T
            halo_fill(late, XM, (g_t[:1], g_t[1:2]), 4)
            halo_fill(late, XP, (g_t[-1:], g_t[-2:-1]), 4)
            for direction in (XM, XP):
                halo_start(early, direction)
                halo_start(late, direction)
        else:
            out[0] = u
        before, after, far = outer_values("gy", *y_ends, sweep, sides)
        v_ym, v_yp = before[:1], after[:1]
        v = g + y_rest[1] * v_ym + y_rest[2] * v_yp
        if more:
            v_t = v.T
            u_ym, u_ym2, *low = halo_wait(early, YM, 4)
            u_yp, u_yp2, *high = halo_wait(early, YP, 4)
            (u_xm2,) = halo_wait(early, XM, 1)
            (u_xp2,) = halo_wait(early, XP, 1)
            p_2, q_2, g_2 = halo_wait(late, YM, 3)
            v_ym2 = jnp.where(has(YM), g_2 + p_2 * far[0][:1] + q_2 * v[:1], 0.0)
            p_2, q_2, g_2 = halo_wait(late, YP, 3)
            v_yp2 = jnp.where(has(YP), g_2 + p_2 * v[-1:] + q_2 * far[1][:1], 0.0)

            def beside(direction, row, lanes):
                p_1, q_1, p_2, q_2, g_1, g_2 = halo_wait(late, direction, 6)
                lo, hi = (
                    [jnp.where(has(direction), end[row : row + 1, n : n + 1], 0.0) for n in lanes]
                    for end in (before, after)
                )
                near = g_1 + p_1 * lo[0] + q_1 * hi[0]
                next_ = g_2 + p_2 * lo[1] + q_2 * hi[1]
                return near, next_, lo[0], hi[0]

            v_xm, v_xm2, mm_v, mp_v = beside(XM, 1, (cx - 1, cx - 2))
            v_xp, v_xp2, pm_v, pp_v = beside(XP, 2, (0, 1))
            mm, mp = (low[0], mm_v), (high[0], mp_v)
            pm, pp = (low[1], pm_v), (high[1], pp_v)
    out[1] = v
    for sweep in range(PASSES):
        for name, ends in gathers:
            for k in range(1, sizes[name]):
                ends_copy(name, ends, sweep, k, me[name]).wait_send()
    for sweep in range(PASSES - 1):
        for ends, sides in zip(y_ends, side_sems):
            for side in (XM, XP):

                @pl.when(has(side))
                def _():
                    for k in range(sizes["gy"]):
                        side_copy(
                            ends, sides, sweep, side, k, me["gy"], side ^ 1
                        ).wait_send()


def on_device(sizes, velocity, wind_stress, thickness, ice_mask, land_mask):
    cy, cx = thickness.shape
    wide = max(cx, cy)
    nx, ny = sizes["gx"], sizes["gy"]
    slots = 2 * PASSES - 1
    dma = pltpu.SemaphoreType.DMA
    strides = (cy - 1).bit_length()
    f32 = jnp.float32
    args = (velocity, wind_stress, thickness, ice_mask, land_mask)
    return pl.pallas_call(
        functools.partial(kernel, sizes),
        out_shape=pltpu.VMEM(velocity.shape, f32),
        in_specs=[pl.BlockSpec(memory_space=pl.ANY)] * 5,
        out_specs=pl.BlockSpec(memory_space=pltpu.VMEM),
        scratch_shapes=[pltpu.VMEM(arg.shape, arg.dtype) for arg in args]
        + [
            dma((5,)),
            pltpu.VMEM((slots, 4, 8, wide), f32),
            pltpu.VMEM((slots, 4, 8, wide), f32),
            pltpu.VMEM((4, 2, wide), f32),
            pltpu.VMEM((4, 2, wide), f32),
            pltpu.VMEM((PASSES, nx, 1, 6, cy), f32),
            pltpu.VMEM((PASSES, nx, 1, 2, cy), f32),
            pltpu.VMEM((PASSES, ny, 3, 6, cx), f32),
            pltpu.VMEM((PASSES, ny, 3, 2, cx), f32),
            pltpu.VMEM((strides, 3, cy, cx), f32),
            pltpu.VMEM((4, cy, cx), f32),
            dma((slots, 4)), dma((slots, 4)), dma((4,)), dma((4,)),
        ]
        + [dma((PASSES, nx - 1))] * 4
        + [dma((PASSES, ny - 1))] * 4
        + [dma((PASSES, 2, ny))] * 4,
        compiler_params=pltpu.CompilerParams(collective_id=0, has_side_effects=True),
        name="ice_relaxation",
    )(*args)


def solution(mesh):
    sizes = {name: int(mesh.shape[name]) for name in ("gx", "gy")}
    cells = P("gy", "gx")
    pairs = P(None, "gy", "gx")
    return jax.shard_map(
        functools.partial(on_device, sizes),
        mesh=mesh,
        in_specs=(pairs, pairs, cells, cells, cells),
        out_specs=pairs,
        check_vma=False,
    )
```
